256 devices in a mesh: dp: 4 (over y), expert: 64 (over z, x, core).
Axes of the slice: x: 4, y: 4, z: 8, core: 2. Of those that a mesh axis runs over, the one named last changes fastest.
Arguments:
- tokens: bfloat16 [32768, 3584], P(('dp', 'expert')), may hold values from -6 to 6
- gate_up: bfloat16 [64, 3584, 2048], P('expert', 'dp'), may hold values from -0.09375 to 0.09375
- down_proj: bfloat16 [64, 1024, 3584], P('expert', None, 'dp'), may hold values from -0.1875 to 0.1875
- expert_ids: int32 [32768, 8], P(('dp', 'expert')), may hold values from 0 to 255, all different within a row; in each aligned block of 128 rows (0 to 127, 128 to 255, ...) at most 8 rows name the same one
- gate_weights: bfloat16 [32768, 8], P(('dp', 'expert')), may hold values from 0.049804688 to 1
Outputs:
- mixed: bfloat16 [32768, 3584], P(('dp', 'expert'))
The draws below stay inside these ranges and needn't reach their ends.
Inputs may be any that keep to these rules, and one draw needn't show every extreme that they name: `expert_ids`: A row names 8 different experts. Among the rows of one device (aligned blocks of 128 rows), no expert is named by more than 8 rows.
All inputs are finite; a program needn't handle non-finite values.
Results may differ from the reference program's by a relative error of at most 0.0058.
Values may be sent and summed in bfloat16 or wider, within the bound.
A program may use at most 128 MiB of HBM per device.

```python
import math
import jax
import jax.numpy as jnp
import numpy as np
from jax import lax

D = 3584
FF = 1024
TOP = 8
TOK_DEV = 128
EXPERTS = 256
COMPUTED = 64
CAP = 8
TOKENS = 32768
N_DP = 4
N_EXPERT = 64


def shard_levels(stream_key, dims, shards, low, high):
    loudness, own = 1.0, jax.random.fold_in(stream_key, 6)
    for position, shards_of in shards:
        heights = jnp.exp(jax.random.uniform(jax.random.fold_in(own, position), (shards_of,), jnp.float32, low / len(shards), high / len(shards)))
        loudness = loudness * jnp.repeat(heights, dims[position] // shards_of).reshape([-1 if axis == position else 1 for axis in range(len(dims))])
    return loudness


def assign_block(rng, own, number, rows, number_of, top, limit, skew):
    ranking = jax.random.permutation(rng, number_of)
    packed, common = shares(number_of, rows * top, limit, skew, True), shares(number_of, rows * top, limit, skew, False)
    places = jnp.arange(number_of)

    def named(sizes, offset_by):
        used = int((sizes > 0).sum())
        fixed = max(1, used // 4)
        shifted = fixed + (places - fixed + offset_by * (used - fixed)) % max(1, number_of - fixed)
        return jnp.zeros((number_of,), jnp.int32).at[ranking[jnp.where(places < fixed, places, shifted)]].set(jnp.asarray(sizes, jnp.int32))

    sizes = jnp.where(number % 4 == 0, named(packed, number // 4), named(common, number - number // 4 - 1))
    mixed = jax.random.permutation(jax.random.fold_in(own, 3), number_of)
    donor, sink = mixed[0:number_of // 2 * 2:2], mixed[1:number_of // 2 * 2:2]
    margin = jnp.minimum(sizes[donor] - 1, limit - sizes[sink]) // 2
    margin = jnp.where((donor == ranking[0]) | (sink == ranking[0]) | (sizes[sink] == 0), 0, jnp.maximum(margin, 0))
    shifted = jax.random.randint(jax.random.fold_in(own, 4), (number_of // 2,), 0, 1 << 20) % (margin + 1)
    sizes = sizes.at[donor].add(-shifted).at[sink].add(shifted)
    members = jnp.searchsorted(jnp.cumsum(sizes), jnp.arange(rows * top), side="right").astype(jnp.int32)
    grid = members.reshape(top, rows).T
    grid = grid[jax.random.permutation(jax.random.fold_in(own, 1), rows)]
    offset_by = jax.random.randint(jax.random.fold_in(own, 2), (rows, 1), 0, top)
    return jnp.take_along_axis(grid, (jnp.arange(top)[None, :] + offset_by) % top, axis=1)


def shares(count, total, limit, skew, full):
    loads = [(1 << 20) // math.isqrt(standing ** skew) + 1 for standing in range(1, count + 1)]
    largest = limit if full else min(limit, max(-(-total // count), total * loads[0] // sum(loads)))
    least = 1 if total - largest >= count - 1 else 0
    counts, spare = [largest] + [least] * (count - 1), total - largest - least * (count - 1)
    while spare > 0:
        candidates = [i for i in range(1, count) if counts[i] < largest] or [i for i in range(1, count) if counts[i] < limit]
        whole, budget = sum([loads[i] for i in candidates]), spare
        for i in candidates:
            addition = min(limit - counts[i], max(1, budget * loads[i] // whole), spare)
            counts[i] = counts[i] + addition
            spare = spare - addition
    return np.array(counts)


def noise(rng, shape, scale, bound, shards=(), kind=jnp.bfloat16):
    drawn = scale * jax.random.normal(rng, shape, jnp.float32)
    if shards:
        drawn = drawn * shard_levels(rng, shape, shards, -0.22, 0.18)
    return jnp.clip(drawn, -bound, bound).astype(kind)


def setup_inputs(seed: int = 0) -> dict:
    arg_keys = jax.random.split(jax.random.key(seed), 6)
    tokens = noise(arg_keys[0], (TOKENS, D), 1.0, 6.0, ((0, 256),))
    gate_up = noise(arg_keys[1], (COMPUTED, D, 2 * FF), D ** -0.5, 0.09375, ((0, 64), (1, 4)))
    down_proj = noise(arg_keys[2], (COMPUTED, FF, D), FF ** -0.5, 0.1875, ((0, 64), (2, 4)))
    expert_ids_keys = jax.random.split(jax.random.fold_in(arg_keys[3], 1), TOKENS // TOK_DEV)
    expert_ids_turns = jax.random.permutation(jax.random.fold_in(arg_keys[3], 3), TOKENS // TOK_DEV)
    expert_ids = jax.vmap(lambda own, number: assign_block(jax.random.fold_in(arg_keys[3], 2), own, number, TOK_DEV, EXPERTS, TOP, CAP, 1))(expert_ids_keys, expert_ids_turns).reshape((TOKENS, TOP))
    gate_weights = jnp.clip(jnp.exp(math.log(1.0) - 2.9996462 * jax.random.uniform(arg_keys[4], (TOKENS, TOP), jnp.float32) ** shard_levels(arg_keys[4], (TOKENS, TOP), ((0, 256),), -0.2, 0.2)), 0.049804688, 1.0).astype(jnp.bfloat16)
    return dict(tokens=tokens, gate_up=gate_up, down_proj=down_proj, expert_ids=expert_ids, gate_weights=gate_weights)


def reference(tokens, gate_up, down_proj, expert_ids, gate_weights):
    most_rows = N_DP * N_EXPERT * CAP
    positions = jnp.arange(most_rows, dtype=jnp.int32)

    def one_expert(total, expert):
        hits = (expert_ids == expert)
        picked = jnp.any(hits, axis=1)
        count = jnp.sum(picked.astype(jnp.int32))
        index = jnp.nonzero(picked, size=most_rows, fill_value=0)[0].astype(jnp.int32)
        valid = positions < count
        weight = jnp.sum(jnp.where(hits[index], gate_weights[index].astype(jnp.float32), 0.0), axis=1)
        weight = jnp.where(valid, weight, 0.0)
        rows = tokens[index]
        weights_gu = lax.dynamic_index_in_dim(gate_up, expert, 0, keepdims=False)
        weights_down = lax.dynamic_index_in_dim(down_proj, expert, 0, keepdims=False)
        gu = jnp.dot(rows, weights_gu, preferred_element_type=jnp.float32)
        hidden = (jax.nn.silu(gu[:, :FF]) * gu[:, FF:]).astype(jnp.bfloat16)
        output = jnp.dot(hidden, weights_down, preferred_element_type=jnp.float32).astype(jnp.bfloat16)
        total = total.at[index].add(weight[:, None] * output.astype(jnp.float32))
        return total, None

    start = jnp.zeros((TOKENS, D), jnp.float32)
    total, unused = lax.scan(one_expert, start, jnp.arange(COMPUTED, dtype=jnp.int32))
    return total.astype(jnp.bfloat16)
```

```python
import functools

import jax
import jax.numpy as jnp
from jax import lax
from jax.experimental import pallas as pl
from jax.experimental.pallas import tpu as pltpu
from jax.sharding import PartitionSpec as P

MESH = pl.DeviceIdType.MESH
NZ, NX = 8, 4
SLOTS = 8
GROUPS = 4
DZ0 = (3, 4, 2, 1)
DZ1 = (5, 0, 6, 7)
GATE_CHUNKS = 7
DOWN_CHUNKS = 2


def kernel(
    tok_ref, gate_hbm, down_hbm, ids_ref, wts_ref, out_ref,
    place, comb, outgoing, rows, rows2, gate, down, acc, hidden, result, returned,
    disp_send, disp_recv, own_copy, gate_send, gate_in, gate_x, gate_sa, gate_sb,
    down_send, down_in, down_x, down_sa, down_sb, ret_send, ret_recv,
):
    p = lax.axis_index("dp")
    e = lax.axis_index("expert")
    z, x, c = e // 8, (e // 2) % 4, e % 2
    m = p // 2
    native = c == m
    foreign = c != m
    sibling = (p, e + 1 - 2 * c)
    pc = p + 1 - 2 * (p % 2)
    cross = (pc, e)
    across = (3 - p, e + 1 - 2 * c)
    home = jnp.where(native, p, 3 - p)
    ff = hidden.shape[1]
    depth = gate.shape[1]
    cols = down.shape[2]

    barrier = pltpu.get_barrier_semaphore()

    @pl.loop(0, 32)
    def _(i):
        ei = ((z + i // 4) % NZ * 4 + (x + i) % NX) * 2

        @pl.when((ei + m != e))
        def _():
            pl.semaphore_signal(barrier, inc=1, device_id=(p, ei + m), device_id_type=MESH)

        pl.semaphore_signal(barrier, inc=1, device_id=(3 - p, ei + m), device_id_type=MESH)
        pl.semaphore_signal(barrier, inc=1, device_id=(home, ei + 1 - m), device_id_type=MESH)

    pl.semaphore_signal(barrier, inc=1, device_id=cross, device_id_type=MESH)

    row = lax.broadcasted_iota(jnp.int32, (512, 128), 0)
    g, ii = row // 128, (row // 8) % 16
    zs, b, dx = ii % 2, (ii // 2) % 2, ii // 4
    dz0 = jnp.where(g == 0, DZ0[0], jnp.where(g == 1, DZ0[1], jnp.where(g == 2, DZ0[2], DZ0[3])))
    dz1 = jnp.where(g == 0, DZ1[0], jnp.where(g == 1, DZ1[1], jnp.where(g == 2, DZ1[2], DZ1[3])))
    dz = jnp.where(zs == 0, dz0, dz1)
    core = jnp.where(b == 0, m, 1 - m)
    expert = ((z + dz) % NZ * 4 + (x + dx) % NX) * 2 + core
    ids = ids_ref[...].T
    wts = wts_ref[...].astype(jnp.float32).T
    named = jnp.zeros((512, 128), jnp.float32)
    weight = jnp.zeros((512, 128), jnp.float32)
    for k in range(8):
        same = expert == ids[k : k + 1, :]
        named = jnp.where(same, 1.0, named)
        weight = jnp.where(same, wts[k : k + 1, :], weight)
    t0 = lax.broadcasted_iota(jnp.int32, (128, 128), 0)
    t1 = lax.broadcasted_iota(jnp.int32, (128, 128), 1)
    earlier = jnp.where(t0 < t1, 1.0, 0.0).astype(jnp.bfloat16)
    before = jnp.dot(named.astype(jnp.bfloat16), earlier, preferred_element_type=jnp.float32)
    slot = (row % 8).astype(jnp.float32)
    chosen = (named > 0.5) & (before == slot)
    place[...] = jnp.where(chosen, 1.0, 0.0).astype(jnp.bfloat16)
    comb[...] = jnp.where(chosen, weight, 0.0).T.astype(jnp.bfloat16)

    @pl.loop(0, 7)
    def _(n):
        at = pl.ds(pl.multiple_of(n * 512, 512), 512)
        block = jnp.dot(place[...], tok_ref[:, at], preferred_element_type=jnp.float32)
        outgoing[:, :, at] = block.astype(jnp.bfloat16).reshape(64, SLOTS, 512)

    pl.semaphore_wait(barrier, jnp.where(native, 96, 97))

    def remote(src, dst, ssem, rsem, to):
        return pltpu.make_async_remote_copy(
            src_ref=src, dst_ref=dst, send_sem=ssem, recv_sem=rsem, device_id=to, device_id_type=MESH
        )

    def piece(ref, k, i, size):
        return ref.at[k, pl.ds(i * size, size), :]

    gsize, dsize = depth // GATE_CHUNKS, ff // DOWN_CHUNKS

    def send_own(hbm, dst, size, chunks, ssem, arrive, to):
        @pl.loop(0, chunks)
        def _(i):
            remote(piece(hbm, 0, i, size), piece(dst, p, i, size), ssem, arrive.at[i], to).start()

    def forward(ref, k, i, size, ssem, arrive, to):
        remote(piece(ref, k, i, size), piece(ref, k, i, size), ssem, arrive.at[i], to).start()

    def arrived(ref, k, i, size, sem):
        pltpu.make_async_copy(piece(ref, k, i, size), piece(ref, k, i, size), sem.at[i]).wait()

    @pl.when(native)
    def _():
        send_own(gate_hbm, gate, gsize, GATE_CHUNKS, gate_send, gate_in, cross)
        send_own(gate_hbm, gate, gsize, GATE_CHUNKS, gate_send, gate_sa, sibling)
        pltpu.make_async_copy(gate_hbm.at[0], gate.at[p], own_copy.at[0]).start()
        pltpu.make_async_copy(down_hbm.at[0], down.at[p], own_copy.at[1]).start()

    @pl.when(foreign)
    def _():
        send_own(gate_hbm, gate, gsize, GATE_CHUNKS, gate_send, gate_in, across)

    for grp in range(GROUPS):

        @pl.loop(0, 16)
        def _(i, grp=grp):
            zsel, bb, ddx = i % 2, (i // 2) % 2, i // 4
            ddz = DZ0[grp] + (DZ1[grp] - DZ0[grp]) * zsel
            to = ((z + ddz) % NZ * 4 + (x + ddx) % NX) * 2 + m
            plane = p + bb * (3 - 2 * p)
            src = outgoing.at[grp * 16 + i]
            dst = rows.at[grp * 16 + i + 2 * (c - bb)]

            def go():
                remote(src, dst, disp_send, disp_recv.at[grp], (plane, to)).start()

            if grp == 1:
                own = native & (i == 1)

                @pl.when(own)
                def _():
                    pltpu.make_async_copy(src, dst, disp_recv.at[grp]).start()

                @pl.when(jnp.logical_not(own))
                def _():
                    go()
            else:
                go()

    @pl.when(native)
    def _():
        send_own(down_hbm, down, dsize, DOWN_CHUNKS, down_send, down_sa, sibling)

        @pl.loop(0, GATE_CHUNKS)
        def _(i):
            arrived(gate, pc, i, gsize, gate_in)
            forward(gate, pc, i, gsize, gate_send, gate_sb, sibling)

        send_own(down_hbm, down, dsize, DOWN_CHUNKS, down_send, down_in, cross)
        pltpu.make_async_copy(gate_hbm.at[0], gate.at[p], own_copy.at[0]).wait()
        pltpu.make_async_copy(down_hbm.at[0], down.at[p], own_copy.at[1]).wait()

    @pl.when(foreign)
    def _():
        @pl.loop(0, GATE_CHUNKS)
        def _(i):
            arrived(gate, 3 - p, i, gsize, gate_in)
            forward(gate, 3 - p, i, gsize, gate_send, gate_x, cross)
            forward(gate, 3 - p, i, gsize, gate_send, gate_sa, sibling)
            arrived(gate, 3 - pc, i, gsize, gate_x)
            forward(gate, 3 - pc, i, gsize, gate_send, gate_sb, sibling)

        send_own(down_hbm, down, dsize, DOWN_CHUNKS, down_send, down_in, across)

    for grp in range(GROUPS):
        part = rows.at[pl.ds(grp * 16, 16)]
        pltpu.make_async_copy(part, part, disp_recv.at[grp]).wait()

        @pl.loop(0, 7)
        def _(n, grp=grp):
            at = pl.ds(pl.multiple_of(n * 512, 512), 512)
            rows2[pl.ds(grp * 128, 128), at] = rows[pl.ds(grp * 16, 16), :, at].reshape(128, 512)

    def gate_part(k, first):
        @pl.loop(0, 8)
        def _(n):
            at = pl.ds(pl.multiple_of(n * 256, 256), 256)
            deep = pl.ds(pl.multiple_of(k * depth, 128), depth)
            part = jnp.dot(rows2[:, deep], gate[k, :, at], preferred_element_type=jnp.float32)
            if first:
                acc[:, at] = part
            else:
                acc[:, at] += part

    def sib_arrived(ref, k, size, chunks, sem):
        @pl.loop(0, chunks)
        def _(i):
            arrived(ref, k, i, size, sem)

    @pl.when(foreign)
    def _():
        sib_arrived(gate, p, gsize, GATE_CHUNKS, gate_sa)
        sib_arrived(gate, pc, gsize, GATE_CHUNKS, gate_sb)

    gate_part(p, True)
    gate_part(pc, False)

    @pl.when(native)
    def _():
        sib_arrived(gate, 3 - p, gsize, GATE_CHUNKS, gate_sa)
        sib_arrived(gate, 3 - pc, gsize, GATE_CHUNKS, gate_sb)

    gate_part(3 - p, False)
    gate_part(3 - pc, False)

    @pl.loop(0, ff // 256)
    def _(n):
        a = acc[:, pl.ds(pl.multiple_of(n * 256, 256), 256)]
        u = acc[:, pl.ds(pl.multiple_of(ff + n * 256, 256), 256)]
        hidden[:, pl.ds(pl.multiple_of(n * 256, 256), 256)] = (a / (1.0 + jnp.exp(-a)) * u).astype(jnp.bfloat16)

    def quarter(k):
        for half in range(2):
            part = jnp.dot(hidden[half * 256 : half * 256 + 256, :], down[k], preferred_element_type=jnp.float32)
            result[k, half * 32 : half * 32 + 32] = part.astype(jnp.bfloat16).reshape(32, SLOTS, cols)
            for grp in (2 * half, 2 * half + 1):

                @pl.loop(0, 16)
                def _(i, grp=grp):
                    zsel, cs, ddx = i % 2, (i // 2) % 2, i // 4
                    ddz = DZ0[grp] + (DZ1[grp] - DZ0[grp]) * zsel
                    to = ((z + NZ - ddz) % NZ * 4 + (x + NX - ddx) % NX) * 2 + cs
                    bb = jnp.where(native, 0, 1)
                    src = result.at[k, grp * 16 + i]
                    dst = returned.at[k, grp * 16 + i + 2 * (bb - cs)]

                    def go():
                        remote(src, dst, ret_send, ret_recv.at[k], (home, to)).start()

                    if grp == 1:
                        own = native & (zsel == 1) & (ddx == 0) & (cs == c)

                        @pl.when(own)
                        def _():
                            pltpu.make_async_copy(src, dst, ret_recv.at[k]).start()

                        @pl.when(jnp.logical_not(own))
                        def _():
                            go()
                    else:
                        go()

    @pl.when(foreign)
    def _():
        sib_arrived(down, p, dsize, DOWN_CHUNKS, down_sa)

    quarter(p)

    @pl.when(native)
    def _():
        @pl.loop(0, DOWN_CHUNKS)
        def _(i):
            arrived(down, pc, i, dsize, down_in)
            forward(down, pc, i, dsize, down_send, down_sb, sibling)

    @pl.when(foreign)
    def _():
        sib_arrived(down, pc, dsize, DOWN_CHUNKS, down_sb)

    quarter(pc)

    @pl.when(foreign)
    def _():
        @pl.loop(0, DOWN_CHUNKS)
        def _(i):
            arrived(down, 3 - p, i, dsize, down_in)
            forward(down, 3 - p, i, dsize, down_send, down_x, cross)
            forward(down, 3 - p, i, dsize, down_send, down_sa, sibling)

    @pl.when(native)
    def _():
        sib_arrived(down, 3 - p, dsize, DOWN_CHUNKS, down_sa)

    quarter(3 - p)

    @pl.when(foreign)
    def _():
        @pl.loop(0, DOWN_CHUNKS)
        def _(i):
            arrived(down, 3 - pc, i, dsize, down_x)
            forward(down, 3 - pc, i, dsize, down_send, down_sb, sibling)

    @pl.when(native)
    def _():
        sib_arrived(down, 3 - pc, dsize, DOWN_CHUNKS, down_sb)

    quarter(3 - pc)

    for k in range(4):
        pltpu.make_async_copy(returned.at[k], returned.at[k], ret_recv.at[k]).wait()
        mixed = jnp.dot(comb[...], returned[k].reshape(512, cols), preferred_element_type=jnp.float32)
        out_ref[:, k * cols : (k + 1) * cols] = mixed.astype(jnp.bfloat16)

    def sent(ref, sem):
        pltpu.make_async_copy(ref, ref, sem).wait()

    @pl.when(native)
    def _():
        sent(outgoing.at[pl.ds(0, 63)], disp_send)
        sent(gate.at[pl.ds(0, 3)], gate_send)
        sent(down.at[pl.ds(0, 3)], down_send)
        sent(result.at[pl.ds(0, 3)], ret_send)
        sent(result.at[3, pl.ds(0, 60)], ret_send)

    @pl.when(foreign)
    def _():
        sent(outgoing, disp_send)
        sent(gate, gate_send)
        sent(down, down_send)
        sent(result, ret_send)


def local(tokens, gate_up, down_proj, expert_ids, gate_weights):
    tok_rows, width = tokens.shape
    _, depth, wide = gate_up.shape
    _, ff, cols = down_proj.shape
    bf, f32 = jnp.bfloat16, jnp.float32
    vmem = pl.BlockSpec(memory_space=pltpu.VMEM)
    hbm = pl.BlockSpec(memory_space=pl.ANY)
    dma = pltpu.SemaphoreType.DMA
    return pl.pallas_call(
        kernel,
        out_shape=jax.ShapeDtypeStruct((tok_rows, width), bf),
        in_specs=[vmem, hbm, hbm, vmem, vmem],
        out_specs=vmem,
        scratch_shapes=[
            pltpu.VMEM((512, 128), bf),
            pltpu.VMEM((128, 512), bf),
            pltpu.VMEM((64, SLOTS, width), bf),
            pltpu.VMEM((64, SLOTS, width), bf),
            pltpu.VMEM((512, width), bf),
            pltpu.VMEM((4, depth, wide), bf),
            pltpu.VMEM((4, ff, cols), bf),
            pltpu.VMEM((512, wide), f32),
            pltpu.VMEM((512, ff), bf),
            pltpu.VMEM((4, 64, SLOTS, cols), bf),
            pltpu.VMEM((4, 64, SLOTS, cols), bf),
            dma, dma((GROUPS,)), dma((2,)),
            dma, dma((GATE_CHUNKS,)), dma((GATE_CHUNKS,)), dma((GATE_CHUNKS,)), dma((GATE_CHUNKS,)),
            dma, dma((DOWN_CHUNKS,)), dma((DOWN_CHUNKS,)), dma((DOWN_CHUNKS,)), dma((DOWN_CHUNKS,)),
            dma, dma((4,)),
        ],
        compiler_params=pltpu.CompilerParams(
            collective_id=0, has_side_effects=True, vmem_limit_bytes=60 * 1024 * 1024
        ),
    )(tokens, gate_up, down_proj, expert_ids, gate_weights)


def solution(mesh):
    placed = (
        P(("dp", "expert"), None),
        P("expert", "dp", None),
        P("expert", None, "dp"),
        P(("dp", "expert"), None),
        P(("dp", "expert"), None),
    )
    return jax.shard_map(
        local, mesh=mesh, in_specs=placed, out_specs=P(("dp", "expert"), None), check_vma=False
    )
```

```python
import functools

import jax
import jax.numpy as jnp
from jax import lax
from jax.experimental import pallas as pl
from jax.experimental.pallas import tpu as pltpu
from jax.sharding import PartitionSpec as P

MESH = pl.DeviceIdType.MESH
NZ, NX = 8, 4
SLOTS = 8
GROUPS = 4
DZ0 = (3, 4, 2, 1)
DZ1 = (5, 0, 6, 7)
GATE_CHUNKS = 7
DOWN_CHUNKS = 4


def kernel(
    tok_ref, gate_hbm, down_hbm, ids_ref, wts_ref, out_ref,
    place, comb, outgoing, rows, rows2, gate, down, acc, hidden, result, returned,
    disp_send, disp_recv, own_copy, gate_send, gate_in, gate_x, gate_sa, gate_sb,
    down_send, down_in, down_x, down_sa, down_sb, ret_send, ret_recv,
):
    p = lax.axis_index("dp")
    e = lax.axis_index("expert")
    z, x, c = e // 8, (e // 2) % 4, e % 2
    m = p // 2
    native = c == m
    foreign = c != m
    sibling = (p, e + 1 - 2 * c)
    pc = p + 1 - 2 * (p % 2)
    cross = (pc, e)
    across = (3 - p, e + 1 - 2 * c)
    home = jnp.where(native, p, 3 - p)
    ff = hidden.shape[1]
    depth = gate.shape[1]
    cols = down.shape[2]

    barrier = pltpu.get_barrier_semaphore()

    def greet(plane, to):
        pl.semaphore_signal(barrier, inc=1, device_id=(plane, to), device_id_type=MESH)

    for ddz in (4, 3, 5, 2, 6, 1, 7, 0):
        for ddx in (2, 1, 3, 0):
            chip = ((z + ddz) % NZ * 4 + (x + ddx) % NX) * 2
            greet(3 - p, chip + m)
            greet(home, chip + 1 - m)
            if ddz or ddx:
                greet(p, chip + m)
    greet(*cross)

    @pl.when(foreign)
    def _():
        greet(*sibling)

    row = lax.broadcasted_iota(jnp.int32, (512, 128), 0)
    g, ii = row // 128, (row // 8) % 16
    zs, b, dx = ii % 2, (ii // 2) % 2, ii // 4
    dz0 = jnp.where(g == 0, DZ0[0], jnp.where(g == 1, DZ0[1], jnp.where(g == 2, DZ0[2], DZ0[3])))
    dz1 = jnp.where(g == 0, DZ1[0], jnp.where(g == 1, DZ1[1], jnp.where(g == 2, DZ1[2], DZ1[3])))
    dz = jnp.where(zs == 0, dz0, dz1)
    core = jnp.where(b == 0, m, 1 - m)
    expert = ((z + dz) % NZ * 4 + (x + dx) % NX) * 2 + core
    ids = ids_ref[...].T
    wts = wts_ref[...].astype(jnp.float32).T
    named = jnp.zeros((512, 128), jnp.float32)
    weight = jnp.zeros((512, 128), jnp.float32)
    for k in range(8):
        same = expert == ids[k : k + 1, :]
        named = jnp.where(same, 1.0, named)
        weight = jnp.where(same, wts[k : k + 1, :], weight)
    t0 = lax.broadcasted_iota(jnp.int32, (128, 128), 0)
    t1 = lax.broadcasted_iota(jnp.int32, (128, 128), 1)
    earlier = jnp.where(t0 < t1, 1.0, 0.0).astype(jnp.bfloat16)
    before = jnp.dot(named.astype(jnp.bfloat16), earlier, preferred_element_type=jnp.float32)
    slot = (row % 8).astype(jnp.float32)
    chosen = (named > 0.5) & (before == slot)
    place[...] = jnp.where(chosen, 1.0, 0.0).astype(jnp.bfloat16)
    comb[...] = jnp.where(chosen, weight, 0.0).T.astype(jnp.bfloat16)

    @pl.loop(0, 7)
    def _(n):
        at = pl.ds(pl.multiple_of(n * 512, 512), 512)
        block = jnp.dot(place[...], tok_ref[:, at], preferred_element_type=jnp.float32)
        outgoing[:, :, at] = block.astype(jnp.bfloat16).reshape(64, SLOTS, 512)

    pl.semaphore_wait(barrier, jnp.where(native, 96, 97))

    def remote(src, dst, ssem, rsem, to):
        return pltpu.make_async_remote_copy(
            src_ref=src, dst_ref=dst, send_sem=ssem, recv_sem=rsem, device_id=to, device_id_type=MESH
        )

    def piece(ref, k, i, size):
        return ref.at[k, pl.ds(i * size, size), :]

    gsize, dsize = depth // GATE_CHUNKS, ff // DOWN_CHUNKS

    def send_own(hbm, dst, size, chunks, ssem, arrive, to):
        @pl.loop(0, chunks)
        def _(i):
            remote(piece(hbm, 0, i, size), piece(dst, p, i, size), ssem, arrive.at[i], to).start()

    def forward(ref, k, i, size, ssem, arrive, to):
        remote(piece(ref, k, i, size), piece(ref, k, i, size), ssem, arrive.at[i], to).start()

    def arrived(ref, k, i, size, sem):
        pltpu.make_async_copy(piece(ref, k, i, size), piece(ref, k, i, size), sem.at[i]).wait()

    @pl.when(native)
    def _():
        send_own(gate_hbm, gate, gsize, GATE_CHUNKS, gate_send, gate_in, cross)
        send_own(gate_hbm, gate, gsize, GATE_CHUNKS, gate_send, gate_sa, sibling)
        pltpu.make_async_copy(gate_hbm.at[0], gate.at[p], own_copy.at[0]).start()
        pltpu.make_async_copy(down_hbm.at[0], down.at[p], own_copy.at[1]).start()

    @pl.when(foreign)
    def _():
        send_own(gate_hbm, gate, gsize, GATE_CHUNKS, gate_send, gate_in, across)

    for grp in range(GROUPS):

        @pl.loop(0, 16)
        def _(i, grp=grp):
            zsel, bb, ddx = i % 2, (i // 2) % 2, i // 4
            ddz = DZ0[grp] + (DZ1[grp] - DZ0[grp]) * zsel
            to = ((z + ddz) % NZ * 4 + (x + ddx) % NX) * 2 + m
            plane = p + bb * (3 - 2 * p)
            src = outgoing.at[grp * 16 + i]
            dst = rows.at[grp * 16 + i + 2 * (c - bb)]

            def go():
                remote(src, dst, disp_send, disp_recv.at[grp], (plane, to)).start()

            if grp == 1:
                own = native & (i == 1)

                @pl.when(own)
                def _():
                    pltpu.make_async_copy(src, dst, disp_recv.at[grp]).start()

                @pl.when(jnp.logical_not(own))
                def _():
                    go()
            else:
                go()

    @pl.when(native)
    def _():
        send_own(down_hbm, down, dsize, DOWN_CHUNKS, down_send, down_sa, sibling)

    def pass_on(i):
        @pl.when(native)
        def _():
            arrived(gate, pc, i, gsize, gate_in)
            forward(gate, pc, i, gsize, gate_send, gate_sb, sibling)

        @pl.when(foreign)
        def _():
            arrived(gate, 3 - p, i, gsize, gate_in)
            forward(gate, 3 - p, i, gsize, gate_send, gate_x, cross)
            forward(gate, 3 - p, i, gsize, gate_send, gate_sa, sibling)
            arrived(gate, 3 - pc, i, gsize, gate_x)
            forward(gate, 3 - pc, i, gsize, gate_send, gate_sb, sibling)

    def from_sibling(ref, k, size, chunks, sem):
        for i in chunks:
            arrived(ref, k, i, size, sem)

    def rows_in(grp):
        part = rows.at[pl.ds(grp * 16, 16)]
        pltpu.make_async_copy(part, part, disp_recv.at[grp]).wait()

        @pl.loop(0, 7)
        def _(n):
            at = pl.ds(pl.multiple_of(n * 512, 512), 512)
            rows2[grp * 128 : grp * 128 + 128, at] = rows[grp * 16 : grp * 16 + 16, :, at].reshape(128, 512)

    def gate_sum(parts, r, at):
        total = None
        for k, k0, kd in parts:
            deep = pl.ds(pl.multiple_of(k * depth + k0, 128), kd)
            term = jnp.dot(rows2[r, deep], gate[k, k0 : k0 + kd, at], preferred_element_type=jnp.float32)
            total = term if total is None else total + term
        return total

    def gate_begin(parts, r):
        @pl.loop(0, 2 * ff // 256)
        def _(n):
            at = pl.ds(pl.multiple_of(n * 256, 256), 256)
            acc[r, at] = gate_sum(parts, r, at)

    def gate_finish(parts, r, begun):
        @pl.loop(0, ff // 256)
        def _(n):
            at = pl.ds(pl.multiple_of(n * 256, 256), 256)
            up = pl.ds(pl.multiple_of(ff + n * 256, 256), 256)
            a, u = gate_sum(parts, r, at), gate_sum(parts, r, up)
            if begun:
                a, u = a + acc[r, at], u + acc[r, up]
            hidden[r, at] = (a / (1.0 + jnp.exp(-a)) * u).astype(jnp.bfloat16)

    early = 5
    cut = early * gsize
    first = [(p, 0, depth), (pc, 0, cut), (3 - p, 0, cut), (3 - pc, 0, cut)]
    last = [(k, cut, depth - cut) for k in (pc, 3 - p, 3 - pc)]
    whole = [(k, 0, depth) for k in (p, pc, 3 - p, 3 - pc)]

    for i in range(early):
        pass_on(i)

    @pl.when(native)
    def _():
        pltpu.make_async_copy(gate_hbm.at[0], gate.at[p], own_copy.at[0]).wait()
        pltpu.make_async_copy(down_hbm.at[0], down.at[p], own_copy.at[1]).wait()
        from_sibling(gate, 3 - p, gsize, range(early), gate_sa)
        from_sibling(gate, 3 - pc, gsize, range(early), gate_sb)

    @pl.when(foreign)
    def _():
        from_sibling(gate, p, gsize, range(GATE_CHUNKS), gate_sa)
        from_sibling(gate, pc, gsize, range(early), gate_sb)

    rows_in(0)
    rows_in(1)
    gate_begin(first, slice(0, 256))
    pass_on(early)
    rows_in(2)
    gate_begin(first, slice(256, 384))
    for i in range(early + 1, GATE_CHUNKS):
        pass_on(i)

    @pl.when(native)
    def _():
        send_own(down_hbm, down, dsize, DOWN_CHUNKS, down_send, down_in, cross)
        from_sibling(gate, 3 - p, gsize, range(early, GATE_CHUNKS), gate_sa)
        from_sibling(gate, 3 - pc, gsize, range(early, GATE_CHUNKS), gate_sb)

    @pl.when(foreign)
    def _():
        send_own(down_hbm, down, dsize, DOWN_CHUNKS, down_send, down_in, across)
        from_sibling(gate, pc, gsize, range(early, GATE_CHUNKS), gate_sb)

    gate_finish(last, slice(0, 384), True)

    def quarter(k, halves):
        for half in halves:
            part = jnp.dot(hidden[half * 256 : half * 256 + 256, :], down[k], preferred_element_type=jnp.float32)
            result[k, half * 32 : half * 32 + 32] = part.astype(jnp.bfloat16).reshape(32, SLOTS, cols)
            for grp in (2 * half, 2 * half + 1):

                @pl.loop(0, 16)
                def _(i, grp=grp):
                    zsel, cs, ddx = i % 2, (i // 2) % 2, i // 4
                    ddz = DZ0[grp] + (DZ1[grp] - DZ0[grp]) * zsel
                    to = ((z + NZ - ddz) % NZ * 4 + (x + NX - ddx) % NX) * 2 + cs
                    bb = jnp.where(native, 0, 1)
                    src = result.at[k, grp * 16 + i]
                    dst = returned.at[k, grp * 16 + i + 2 * (bb - cs)]

                    def go():
                        remote(src, dst, ret_send, ret_recv.at[k], (home, to)).start()

                    if grp == 1:
                        own = native & (zsel == 1) & (ddx == 0) & (cs == c)

                        @pl.when(own)
                        def _():
                            pltpu.make_async_copy(src, dst, ret_recv.at[k]).start()

                        @pl.when(jnp.logical_not(own))
                        def _():
                            go()
                    else:
                        go()

    @pl.when(foreign)
    def _():
        from_sibling(down, p, dsize, range(DOWN_CHUNKS), down_sa)

    quarter(p, (0,))
    rows_in(3)
    gate_finish(whole, slice(384, 512), False)
    quarter(p, (1,))

    @pl.when(native)
    def _():
        for i in range(DOWN_CHUNKS):
            arrived(down, pc, i, dsize, down_in)
            forward(down, pc, i, dsize, down_send, down_sb, sibling)

    @pl.when(foreign)
    def _():
        for i in range(DOWN_CHUNKS):
            arrived(down, 3 - p, i, dsize, down_in)
            forward(down, 3 - p, i, dsize, down_send, down_x, cross)
            forward(down, 3 - p, i, dsize, down_send, down_sa, sibling)

    quarter(jnp.where(native, pc, 3 - p), (0, 1))

    @pl.when(native)
    def _():
        from_sibling(down, 3 - p, dsize, range(DOWN_CHUNKS), down_sa)

    @pl.when(foreign)
    def _():
        from_sibling(down, pc, dsize, range(DOWN_CHUNKS), down_sb)

    quarter(jnp.where(native, 3 - p, pc), (0, 1))

    @pl.when(foreign)
    def _():
        for i in range(DOWN_CHUNKS):
            arrived(down, 3 - pc, i, dsize, down_x)
            forward(down, 3 - pc, i, dsize, down_send, down_sb, sibling)

    @pl.when(native)
    def _():
        from_sibling(down, 3 - pc, dsize, range(DOWN_CHUNKS), down_sb)

    quarter(3 - pc, (0, 1))

    for k in range(4):
        pltpu.make_async_copy(returned.at[k], returned.at[k], ret_recv.at[k]).wait()
        mixed = jnp.dot(comb[...], returned[k].reshape(512, cols), preferred_element_type=jnp.float32)
        out_ref[:, k * cols : (k + 1) * cols] = mixed.astype(jnp.bfloat16)

    def sent(ref, sem):
        pltpu.make_async_copy(ref, ref, sem).wait()

    @pl.when(native)
    def _():
        sent(outgoing.at[pl.ds(0, 63)], disp_send)
        sent(gate.at[pl.ds(0, 3)], gate_send)
        sent(down.at[pl.ds(0, 3)], down_send)
        sent(result.at[pl.ds(0, 3)], ret_send)
        sent(result.at[3, pl.ds(0, 60)], ret_send)

    @pl.when(foreign)
    def _():
        sent(outgoing, disp_send)
        sent(gate, gate_send)
        sent(down, down_send)
        sent(result, ret_send)


def local(tokens, gate_up, down_proj, expert_ids, gate_weights):
    tok_rows, width = tokens.shape
    _, depth, wide = gate_up.shape
    _, ff, cols = down_proj.shape
    bf, f32 = jnp.bfloat16, jnp.float32
    vmem = pl.BlockSpec(memory_space=pltpu.VMEM)
    hbm = pl.BlockSpec(memory_space=pl.ANY)
    dma = pltpu.SemaphoreType.DMA
    return pl.pallas_call(
        kernel,
        out_shape=jax.ShapeDtypeStruct((tok_rows, width), bf),
        in_specs=[vmem, hbm, hbm, vmem, vmem],
        out_specs=vmem,
        scratch_shapes=[
            pltpu.VMEM((512, 128), bf),
            pltpu.VMEM((128, 512), bf),
            pltpu.VMEM((64, SLOTS, width), bf),
            pltpu.VMEM((64, SLOTS, width), bf),
            pltpu.VMEM((512, width), bf),
            pltpu.VMEM((4, depth, wide), bf),
            pltpu.VMEM((4, ff, cols), bf),
            pltpu.VMEM((512, wide), f32),
            pltpu.VMEM((512, ff), bf),
            pltpu.VMEM((4, 64, SLOTS, cols), bf),
            pltpu.VMEM((4, 64, SLOTS, cols), bf),
            dma, dma((GROUPS,)), dma((2,)),
            dma, dma((GATE_CHUNKS,)), dma((GATE_CHUNKS,)), dma((GATE_CHUNKS,)), dma((GATE_CHUNKS,)),
            dma, dma((DOWN_CHUNKS,)), dma((DOWN_CHUNKS,)), dma((DOWN_CHUNKS,)), dma((DOWN_CHUNKS,)),
            dma, dma((4,)),
        ],
        compiler_params=pltpu.CompilerParams(
            collective_id=0, has_side_effects=True, vmem_limit_bytes=60 * 1024 * 1024
        ),
    )(tokens, gate_up, down_proj, expert_ids, gate_weights)


def solution(mesh):
    placed = (
        P(("dp", "expert"), None),
        P("expert", "dp", None),
        P("expert", None, "dp"),
        P(("dp", "expert"), None),
        P(("dp", "expert"), None),
    )
    return jax.shard_map(
        local, mesh=mesh, in_specs=placed, out_specs=P(("dp", "expert"), None), check_vma=False
    )
```

```python
import functools

import jax
import jax.numpy as jnp
from jax import lax
from jax.experimental import pallas as pl
from jax.experimental.pallas import tpu as pltpu
from jax.sharding import PartitionSpec as P

MESH = pl.DeviceIdType.MESH
NZ, NX = 8, 4
SLOTS = 8
GROUPS = 4
DZ0 = (3, 4, 2, 1)
DZ1 = (5, 0, 6, 7)
GATE_CHUNKS = 7
DOWN_CHUNKS = 4
AHEAD = 7
LAG = 1
DISPATCH = ((0,), (1,), (), (2,), (3,), (), (), ())


def kernel(
    tok_ref, gate_hbm, down_hbm, ids_ref, wts_ref, out_ref,
    place, comb, outgoing, rows, rows2, gate, down, acc, hidden, result, returned,
    disp_send, disp_recv, own_copy, gate_send, gate_in, gate_x, gate_sa, gate_sb,
    down_send, down_in, down_x, down_sa, down_sb, ret_send, ret_recv,
):
    p = lax.axis_index("dp")
    e = lax.axis_index("expert")
    z, x, c = e // 8, (e // 2) % 4, e % 2
    m = p // 2
    native = c == m
    foreign = c != m
    sibling = (p, e + 1 - 2 * c)
    pc = p + 1 - 2 * (p % 2)
    cross = (pc, e)
    across = (3 - p, e + 1 - 2 * c)
    home = jnp.where(native, p, 3 - p)
    ff = hidden.shape[1]
    depth = gate.shape[1]
    cols = down.shape[2]

    barrier = pltpu.get_barrier_semaphore()

    def greet(plane, to):
        pl.semaphore_signal(barrier, inc=1, device_id=(plane, to), device_id_type=MESH)

    for ddz in (4, 3, 5, 2, 6, 1, 7, 0):
        for ddx in (2, 1, 3, 0):
            chip = ((z + ddz) % NZ * 4 + (x + ddx) % NX) * 2
            greet(3 - p, chip + m)
            greet(home, chip + 1 - m)
            if ddz or ddx:
                greet(p, chip + m)
    greet(*cross)

    @pl.when(foreign)
    def _():
        greet(*sibling)

    row = lax.broadcasted_iota(jnp.int32, (512, 128), 0)
    g, ii = row // 128, (row // 8) % 16
    zs, b, dx = ii % 2, (ii // 2) % 2, ii // 4
    dz0 = jnp.where(g == 0, DZ0[0], jnp.where(g == 1, DZ0[1], jnp.where(g == 2, DZ0[2], DZ0[3])))
    dz1 = jnp.where(g == 0, DZ1[0], jnp.where(g == 1, DZ1[1], jnp.where(g == 2, DZ1[2], DZ1[3])))
    dz = jnp.where(zs == 0, dz0, dz1)
    core = jnp.where(b == 0, m, 1 - m)
    expert = ((z + dz) % NZ * 4 + (x + dx) % NX) * 2 + core
    ids = ids_ref[...].T
    wts = wts_ref[...].astype(jnp.float32).T
    named = jnp.zeros((512, 128), jnp.float32)
    weight = jnp.zeros((512, 128), jnp.float32)
    for k in range(8):
        same = expert == ids[k : k + 1, :]
        named = jnp.where(same, 1.0, named)
        weight = jnp.where(same, wts[k : k + 1, :], weight)
    t0 = lax.broadcasted_iota(jnp.int32, (128, 128), 0)
    t1 = lax.broadcasted_iota(jnp.int32, (128, 128), 1)
    earlier = jnp.where(t0 < t1, 1.0, 0.0).astype(jnp.bfloat16)
    before = jnp.dot(named.astype(jnp.bfloat16), earlier, preferred_element_type=jnp.float32)
    slot = (row % 8).astype(jnp.float32)
    chosen = (named > 0.5) & (before == slot)
    place[...] = jnp.where(chosen, 1.0, 0.0).astype(jnp.bfloat16)
    comb[...] = jnp.where(chosen, weight, 0.0).T.astype(jnp.bfloat16)

    @pl.loop(0, 7)
    def _(n):
        at = pl.ds(pl.multiple_of(n * 512, 512), 512)
        block = jnp.dot(place[...], tok_ref[:, at], preferred_element_type=jnp.float32)
        outgoing[:, :, at] = block.astype(jnp.bfloat16).reshape(64, SLOTS, 512)

    pl.semaphore_wait(barrier, jnp.where(native, 96, 97))

    def remote(src, dst, ssem, rsem, to):
        return pltpu.make_async_remote_copy(
            src_ref=src, dst_ref=dst, send_sem=ssem, recv_sem=rsem, device_id=to, device_id_type=MESH
        )

    def piece(ref, k, i, size):
        return ref.at[k, pl.ds(i * size, size), :]

    gsize, dsize = depth // GATE_CHUNKS, ff // DOWN_CHUNKS

    def send_own(hbm, dst, size, chunks, ssem, arrive, to):
        for i in chunks:
            remote(piece(hbm, 0, i, size), piece(dst, p, i, size), ssem, arrive.at[i], to).start()

    def forward(ref, k, i, size, ssem, arrive, to):
        remote(piece(ref, k, i, size), piece(ref, k, i, size), ssem, arrive.at[i], to).start()

    def arrived(ref, k, i, size, sem):
        pltpu.make_async_copy(piece(ref, k, i, size), piece(ref, k, i, size), sem.at[i]).wait()

    def send_gate(chunks):
        @pl.when(native)
        def _():
            send_own(gate_hbm, gate, gsize, chunks, gate_send, gate_in, cross)
            send_own(gate_hbm, gate, gsize, chunks, gate_send, gate_sa, sibling)

        @pl.when(foreign)
        def _():
            send_own(gate_hbm, gate, gsize, chunks, gate_send, gate_in, across)

    send_gate(range(AHEAD))

    def dispatch(grp):
        @pl.loop(0, 16)
        def _(i):
            zsel, bb, ddx = i % 2, (i // 2) % 2, i // 4
            ddz = DZ0[grp] + (DZ1[grp] - DZ0[grp]) * zsel
            to = ((z + ddz) % NZ * 4 + (x + ddx) % NX) * 2 + m
            plane = p + bb * (3 - 2 * p)
            src = outgoing.at[grp * 16 + i]
            dst = rows.at[grp * 16 + i + 2 * (c - bb)]

            def go():
                remote(src, dst, disp_send, disp_recv.at[grp], (plane, to)).start()

            if grp == 1:
                own = native & (i == 1)

                @pl.when(own)
                def _():
                    pltpu.make_async_copy(src, dst, disp_recv.at[grp]).start()

                @pl.when(jnp.logical_not(own))
                def _():
                    go()
            else:
                go()

    for grp in DISPATCH[0]:
        dispatch(grp)

    @pl.when(native)
    def _():
        pltpu.make_async_copy(gate_hbm.at[0], gate.at[p], own_copy.at[0]).start()
        pltpu.make_async_copy(down_hbm.at[0], down.at[p], own_copy.at[1]).start()
        send_own(down_hbm, down, dsize, range(DOWN_CHUNKS), down_send, down_sa, sibling)

    def share_far(i):
        arrived(gate, 3 - pc, i, gsize, gate_x)
        forward(gate, 3 - pc, i, gsize, gate_send, gate_sb, sibling)

    def pass_on(i):
        if i + AHEAD < GATE_CHUNKS:
            send_gate([i + AHEAD])

        @pl.when(native)
        def _():
            arrived(gate, pc, i, gsize, gate_in)
            forward(gate, pc, i, gsize, gate_send, gate_sb, sibling)

        @pl.when(foreign)
        def _():
            arrived(gate, 3 - p, i, gsize, gate_in)
            forward(gate, 3 - p, i, gsize, gate_send, gate_x, cross)
            forward(gate, 3 - p, i, gsize, gate_send, gate_sa, sibling)
            if i >= LAG:
                share_far(i - LAG)

        for grp in DISPATCH[i + 1]:
            dispatch(grp)

    def send_down():
        @pl.when(native)
        def _():
            send_own(down_hbm, down, dsize, range(DOWN_CHUNKS), down_send, down_in, cross)

        @pl.when(foreign)
        def _():
            send_own(down_hbm, down, dsize, range(DOWN_CHUNKS), down_send, down_in, across)

    def from_sibling(ref, k, size, chunks, sem):
        for i in chunks:
            arrived(ref, k, i, size, sem)

    def rows_in(grp):
        part = rows.at[pl.ds(grp * 16, 16)]
        pltpu.make_async_copy(part, part, disp_recv.at[grp]).wait()

        @pl.loop(0, 7)
        def _(n):
            at = pl.ds(pl.multiple_of(n * 512, 512), 512)
            rows2[grp * 128 : grp * 128 + 128, at] = rows[grp * 16 : grp * 16 + 16, :, at].reshape(128, 512)

    def gate_sum(parts, r, at):
        total = None
        for k, k0, kd in parts:
            deep = pl.ds(pl.multiple_of(k * depth + k0, 128), kd)
            term = jnp.dot(rows2[r, deep], gate[k, k0 : k0 + kd, at], preferred_element_type=jnp.float32)
            total = term if total is None else total + term
        return total

    def gate_begin(parts, r):
        @pl.loop(0, 2 * ff // 256)
        def _(n):
            at = pl.ds(pl.multiple_of(n * 256, 256), 256)
            acc[r, at] = gate_sum(parts, r, at)

    def gate_finish(parts, r, begun):
        @pl.loop(0, ff // 256)
        def _(n):
            at = pl.ds(pl.multiple_of(n * 256, 256), 256)
            up = pl.ds(pl.multiple_of(ff + n * 256, 256), 256)
            a, u = gate_sum(parts, r, at), gate_sum(parts, r, up)
            if begun:
                a, u = a + acc[r, at], u + acc[r, up]
            hidden[r, at] = (a / (1.0 + jnp.exp(-a)) * u).astype(jnp.bfloat16)

    early = GATE_CHUNKS - 1
    cut = early * gsize
    far = (early - LAG) * gsize
    first = [(p, 0, depth), (pc, 0, cut), (3 - p, 0, cut), (3 - pc, 0, far)]
    last = [(pc, cut, depth - cut), (3 - p, cut, depth - cut), (3 - pc, far, depth - far)]
    whole = [(k, 0, depth) for k in (p, pc, 3 - p, 3 - pc)]

    for i in range(early):
        pass_on(i)

    @pl.when(native)
    def _():
        pltpu.make_async_copy(gate_hbm.at[0], gate.at[p], own_copy.at[0]).wait()
        pltpu.make_async_copy(down_hbm.at[0], down.at[p], own_copy.at[1]).wait()
        from_sibling(gate, 3 - p, gsize, range(early), gate_sa)
        from_sibling(gate, 3 - pc, gsize, range(early - LAG), gate_sb)

    @pl.when(foreign)
    def _():
        from_sibling(gate, p, gsize, range(GATE_CHUNKS), gate_sa)
        from_sibling(gate, pc, gsize, range(early), gate_sb)

    rows_in(0)
    rows_in(1)
    gate_begin(first, slice(0, 256))
    send_down()

    for i in range(early, GATE_CHUNKS):
        pass_on(i)

    @pl.when(native)
    def _():
        from_sibling(gate, 3 - p, gsize, range(early, GATE_CHUNKS), gate_sa)
        from_sibling(gate, 3 - pc, gsize, range(early - LAG, GATE_CHUNKS), gate_sb)

    @pl.when(foreign)
    def _():
        for i in range(GATE_CHUNKS - LAG, GATE_CHUNKS):
            share_far(i)
        from_sibling(gate, pc, gsize, range(early, GATE_CHUNKS), gate_sb)

    gate_finish(last, slice(0, 256), True)

    def quarter(k, halves):
        for half in halves:
            part = jnp.dot(hidden[half * 256 : half * 256 + 256, :], down[k], preferred_element_type=jnp.float32)
            result[k, half * 32 : half * 32 + 32] = part.astype(jnp.bfloat16).reshape(32, SLOTS, cols)
            for grp in (2 * half, 2 * half + 1):

                @pl.loop(0, 16)
                def _(i, grp=grp):
                    zsel, cs, ddx = i % 2, (i // 2) % 2, i // 4
                    ddz = DZ0[grp] + (DZ1[grp] - DZ0[grp]) * zsel
                    to = ((z + NZ - ddz) % NZ * 4 + (x + NX - ddx) % NX) * 2 + cs
                    bb = jnp.where(native, 0, 1)
                    src = result.at[k, grp * 16 + i]
                    dst = returned.at[k, grp * 16 + i + 2 * (bb - cs)]

                    def go():
                        remote(src, dst, ret_send, ret_recv.at[k], (home, to)).start()

                    if grp == 1:
                        own = native & (zsel == 1) & (ddx == 0) & (cs == c)

                        @pl.when(own)
                        def _():
                            pltpu.make_async_copy(src, dst, ret_recv.at[k]).start()

                        @pl.when(jnp.logical_not(own))
                        def _():
                            go()
                    else:
                        go()

    @pl.when(foreign)
    def _():
        from_sibling(down, p, dsize, range(DOWN_CHUNKS), down_sa)

    quarter(p, (0,))
    rows_in(2)
    rows_in(3)
    gate_finish(whole, slice(256, 512), False)
    quarter(p, (1,))

    def pass_down(chunks):
        for i in chunks:
            arrived(down, 3 - p, i, dsize, down_in)
            forward(down, 3 - p, i, dsize, down_send, down_x, cross)
            forward(down, 3 - p, i, dsize, down_send, down_sa, sibling)

    half = DOWN_CHUNKS // 2

    @pl.when(native)
    def _():
        for i in range(DOWN_CHUNKS):
            arrived(down, pc, i, dsize, down_in)
            forward(down, pc, i, dsize, down_send, down_sb, sibling)

    @pl.when(foreign)
    def _():
        pass_down(range(half))
        from_sibling(down, pc, dsize, range(DOWN_CHUNKS), down_sb)

    quarter(pc, (0, 1))

    @pl.when(native)
    def _():
        from_sibling(down, 3 - p, dsize, range(DOWN_CHUNKS), down_sa)

    @pl.when(foreign)
    def _():
        pass_down(range(half, DOWN_CHUNKS))

    quarter(3 - p, (0, 1))

    @pl.when(foreign)
    def _():
        for i in range(DOWN_CHUNKS):
            arrived(down, 3 - pc, i, dsize, down_x)
            forward(down, 3 - pc, i, dsize, down_send, down_sb, sibling)

    @pl.when(native)
    def _():
        from_sibling(down, 3 - pc, dsize, range(DOWN_CHUNKS), down_sb)

    quarter(3 - pc, (0, 1))

    for k in range(4):
        pltpu.make_async_copy(returned.at[k], returned.at[k], ret_recv.at[k]).wait()
        mixed = jnp.dot(comb[...], returned[k].reshape(512, cols), preferred_element_type=jnp.float32)
        out_ref[:, k * cols : (k + 1) * cols] = mixed.astype(jnp.bfloat16)

    def sent(ref, sem):
        pltpu.make_async_copy(ref, ref, sem).wait()

    @pl.when(native)
    def _():
        sent(outgoing.at[pl.ds(0, 63)], disp_send)
        sent(gate.at[pl.ds(0, 3)], gate_send)
        sent(down.at[pl.ds(0, 3)], down_send)
        sent(result.at[pl.ds(0, 3)], ret_send)
        sent(result.at[3, pl.ds(0, 60)], ret_send)

    @pl.when(foreign)
    def _():
        sent(outgoing, disp_send)
        sent(gate, gate_send)
        sent(down, down_send)
        sent(result, ret_send)


def local(tokens, gate_up, down_proj, expert_ids, gate_weights):
    tok_rows, width = tokens.shape
    _, depth, wide = gate_up.shape
    _, ff, cols = down_proj.shape
    bf, f32 = jnp.bfloat16, jnp.float32
    vmem = pl.BlockSpec(memory_space=pltpu.VMEM)
    hbm = pl.BlockSpec(memory_space=pl.ANY)
    dma = pltpu.SemaphoreType.DMA
    return pl.pallas_call(
        kernel,
        out_shape=jax.ShapeDtypeStruct((tok_rows, width), bf),
        in_specs=[vmem, hbm, hbm, vmem, vmem],
        out_specs=vmem,
        scratch_shapes=[
            pltpu.VMEM((512, 128), bf),
            pltpu.VMEM((128, 512), bf),
            pltpu.VMEM((64, SLOTS, width), bf),
            pltpu.VMEM((64, SLOTS, width), bf),
            pltpu.VMEM((512, width), bf),
            pltpu.VMEM((4, depth, wide), bf),
            pltpu.VMEM((4, ff, cols), bf),
            pltpu.VMEM((512, wide), f32),
            pltpu.VMEM((512, ff), bf),
            pltpu.VMEM((4, 64, SLOTS, cols), bf),
            pltpu.VMEM((4, 64, SLOTS, cols), bf),
            dma, dma((GROUPS,)), dma((2,)),
            dma, dma((GATE_CHUNKS,)), dma((GATE_CHUNKS,)), dma((GATE_CHUNKS,)), dma((GATE_CHUNKS,)),
            dma, dma((DOWN_CHUNKS,)), dma((DOWN_CHUNKS,)), dma((DOWN_CHUNKS,)), dma((DOWN_CHUNKS,)),
            dma, dma((4,)),
        ],
        compiler_params=pltpu.CompilerParams(
            collective_id=0, has_side_effects=True, vmem_limit_bytes=60 * 1024 * 1024
        ),
    )(tokens, gate_up, down_proj, expert_ids, gate_weights)


def solution(mesh):
    placed = (
        P(("dp", "expert"), None),
        P("expert", "dp", None),
        P("expert", None, "dp"),
        P(("dp", "expert"), None),
        P(("dp", "expert"), None),
    )
    return jax.shard_map(
        local, mesh=mesh, in_specs=placed, out_specs=P(("dp", "expert"), None), check_vma=False
    )
```

```python
import functools

import jax
import jax.numpy as jnp
from jax import lax
from jax.experimental import pallas as pl
from jax.experimental.pallas import tpu as pltpu
from jax.sharding import PartitionSpec as P

MESH = pl.DeviceIdType.MESH
NZ, NX = 8, 4
SLOTS = 8
GROUPS = 4
DZ0 = (3, 4, 2, 1)
DZ1 = (5, 0, 6, 7)
GATE_CHUNKS = 7
DOWN_CHUNKS = 4
AHEAD = 7
LAG = 1
DISPATCH = ((0,), (1,), (), (2,), (3,), (), (), ())


def kernel(
    tok_ref, gate_hbm, down_hbm, ids_ref, wts_ref, out_ref,
    place, comb, outgoing, rows, rows2, gate, down, acc, hidden, result, returned,
    disp_send, disp_recv, own_copy, gate_send, gate_in, gate_x, gate_sa, gate_sb,
    down_send, down_in, down_x, down_sa, down_sb, ret_send, ret_recv,
):
    p = lax.axis_index("dp")
    e = lax.axis_index("expert")
    z, x, c = e // 8, (e // 2) % 4, e % 2
    m = p // 2
    native = c == m
    foreign = c != m
    sibling = (p, e + 1 - 2 * c)
    pc = p + 1 - 2 * (p % 2)
    cross = (pc, e)
    across = (3 - p, e + 1 - 2 * c)
    home = jnp.where(native, p, 3 - p)
    ff = hidden.shape[1]
    depth = gate.shape[1]
    cols = down.shape[2]

    barrier = pltpu.get_barrier_semaphore()

    def greet(plane, to):
        pl.semaphore_signal(barrier, inc=1, device_id=(plane, to), device_id_type=MESH)

    for ddz in (4, 3, 5, 2, 6, 1, 7, 0):
        for ddx in (2, 1, 3, 0):
            chip = ((z + ddz) % NZ * 4 + (x + ddx) % NX) * 2
            greet(3 - p, chip + m)
            greet(home, chip + 1 - m)
            if ddz or ddx:
                greet(p, chip + m)
    greet(*cross)

    @pl.when(foreign)
    def _():
        greet(*sibling)

    row = lax.broadcasted_iota(jnp.int32, (512, 128), 0)
    g, ii = row // 128, (row // 8) % 16
    zs, b, dx = ii % 2, (ii // 2) % 2, ii // 4
    dz0 = jnp.where(g == 0, DZ0[0], jnp.where(g == 1, DZ0[1], jnp.where(g == 2, DZ0[2], DZ0[3])))
    dz1 = jnp.where(g == 0, DZ1[0], jnp.where(g == 1, DZ1[1], jnp.where(g == 2, DZ1[2], DZ1[3])))
    dz = jnp.where(zs == 0, dz0, dz1)
    core = jnp.where(b == 0, m, 1 - m)
    expert = ((z + dz) % NZ * 4 + (x + dx) % NX) * 2 + core
    ids = ids_ref[...].T
    wts = wts_ref[...].astype(jnp.float32).T
    named = jnp.zeros((512, 128), jnp.float32)
    weight = jnp.zeros((512, 128), jnp.float32)
    for k in range(8):
        same = expert == ids[k : k + 1, :]
        named = jnp.where(same, 1.0, named)
        weight = jnp.where(same, wts[k : k + 1, :], weight)
    t0 = lax.broadcasted_iota(jnp.int32, (128, 128), 0)
    t1 = lax.broadcasted_iota(jnp.int32, (128, 128), 1)
    earlier = jnp.where(t0 < t1, 1.0, 0.0).astype(jnp.bfloat16)
    before = jnp.dot(named.astype(jnp.bfloat16), earlier, preferred_element_type=jnp.float32)
    slot = (row % 8).astype(jnp.float32)
    chosen = (named > 0.5) & (before == slot)
    place[...] = jnp.where(chosen, 1.0, 0.0).astype(jnp.bfloat16)
    comb[...] = jnp.where(chosen, weight, 0.0).T.astype(jnp.bfloat16)

    def pick(r0, r1):
        @pl.loop(0, 7)
        def _(n):
            at = pl.ds(pl.multiple_of(n * 512, 512), 512)
            block = jnp.dot(place[r0:r1, :], tok_ref[:, at], preferred_element_type=jnp.float32)
            outgoing[r0 // 8 : r1 // 8, :, at] = block.astype(jnp.bfloat16).reshape((r1 - r0) // 8, SLOTS, 512)

    pick(0, 128)
    pl.semaphore_wait(barrier, jnp.where(native, 96, 97))

    def remote(src, dst, ssem, rsem, to):
        return pltpu.make_async_remote_copy(
            src_ref=src, dst_ref=dst, send_sem=ssem, recv_sem=rsem, device_id=to, device_id_type=MESH
        )

    def piece(ref, k, i, size):
        return ref.at[k, pl.ds(i * size, size), :]

    gsize, dsize = depth // GATE_CHUNKS, ff // DOWN_CHUNKS

    def send_own(hbm, dst, size, chunks, ssem, arrive, to):
        for i in chunks:
            remote(piece(hbm, 0, i, size), piece(dst, p, i, size), ssem, arrive.at[i], to).start()

    def forward(ref, k, i, size, ssem, arrive, to):
        remote(piece(ref, k, i, size), piece(ref, k, i, size), ssem, arrive.at[i], to).start()

    def arrived(ref, k, i, size, sem):
        pltpu.make_async_copy(piece(ref, k, i, size), piece(ref, k, i, size), sem.at[i]).wait()

    def send_gate(chunks):
        @pl.when(native)
        def _():
            send_own(gate_hbm, gate, gsize, chunks, gate_send, gate_in, cross)
            send_own(gate_hbm, gate, gsize, chunks, gate_send, gate_sa, sibling)

        @pl.when(foreign)
        def _():
            send_own(gate_hbm, gate, gsize, chunks, gate_send, gate_in, across)

    send_gate(range(AHEAD))

    def dispatch(grp):
        @pl.loop(0, 16)
        def _(i):
            zsel, bb, ddx = i % 2, (i // 2) % 2, i // 4
            ddz = DZ0[grp] + (DZ1[grp] - DZ0[grp]) * zsel
            to = ((z + ddz) % NZ * 4 + (x + ddx) % NX) * 2 + m
            plane = p + bb * (3 - 2 * p)
            src = outgoing.at[grp * 16 + i]
            dst = rows.at[grp * 16 + i + 2 * (c - bb)]

            def go():
                remote(src, dst, disp_send, disp_recv.at[grp], (plane, to)).start()

            if grp == 1:
                own = native & (i == 1)

                @pl.when(own)
                def _():
                    pltpu.make_async_copy(src, dst, disp_recv.at[grp]).start()

                @pl.when(jnp.logical_not(own))
                def _():
                    go()
            else:
                go()

    dispatch(0)
    pick(128, 512)
    for grp in DISPATCH[0][1:]:
        dispatch(grp)

    @pl.when(native)
    def _():
        pltpu.make_async_copy(gate_hbm.at[0], gate.at[p], own_copy.at[0]).start()
        pltpu.make_async_copy(down_hbm.at[0], down.at[p], own_copy.at[1]).start()
        send_own(down_hbm, down, dsize, range(DOWN_CHUNKS), down_send, down_sa, sibling)

    def share_far(i):
        arrived(gate, 3 - pc, i, gsize, gate_x)
        forward(gate, 3 - pc, i, gsize, gate_send, gate_sb, sibling)

    def pass_on(i):
        if i + AHEAD < GATE_CHUNKS:
            send_gate([i + AHEAD])

        @pl.when(native)
        def _():
            arrived(gate, pc, i, gsize, gate_in)
            forward(gate, pc, i, gsize, gate_send, gate_sb, sibling)

        @pl.when(foreign)
        def _():
            arrived(gate, 3 - p, i, gsize, gate_in)
            forward(gate, 3 - p, i, gsize, gate_send, gate_x, cross)
            forward(gate, 3 - p, i, gsize, gate_send, gate_sa, sibling)
            if i >= LAG:
                share_far(i - LAG)

        for grp in DISPATCH[i + 1]:
            dispatch(grp)

    def send_down():
        @pl.when(native)
        def _():
            send_own(down_hbm, down, dsize, range(DOWN_CHUNKS), down_send, down_in, cross)

        @pl.when(foreign)
        def _():
            send_own(down_hbm, down, dsize, range(DOWN_CHUNKS), down_send, down_in, across)

    def from_sibling(ref, k, size, chunks, sem):
        for i in chunks:
            arrived(ref, k, i, size, sem)

    def rows_in(grp):
        part = rows.at[pl.ds(grp * 16, 16)]
        pltpu.make_async_copy(part, part, disp_recv.at[grp]).wait()

        @pl.loop(0, 7)
        def _(n):
            at = pl.ds(pl.multiple_of(n * 512, 512), 512)
            rows2[grp * 128 : grp * 128 + 128, at] = rows[grp * 16 : grp * 16 + 16, :, at].reshape(128, 512)

    def gate_sum(parts, r, at):
        total = None
        for k, k0, kd in parts:
            deep = pl.ds(pl.multiple_of(k * depth + k0, 128), kd)
            term = jnp.dot(rows2[r, deep], gate[k, k0 : k0 + kd, at], preferred_element_type=jnp.float32)
            total = term if total is None else total + term
        return total

    def gate_begin(parts, r):
        @pl.loop(0, 2 * ff // 256)
        def _(n):
            at = pl.ds(pl.multiple_of(n * 256, 256), 256)
            acc[r, at] = gate_sum(parts, r, at)

    def gate_finish(parts, r, begun):
        @pl.loop(0, ff // 256)
        def _(n):
            at = pl.ds(pl.multiple_of(n * 256, 256), 256)
            up = pl.ds(pl.multiple_of(ff + n * 256, 256), 256)
            a, u = gate_sum(parts, r, at), gate_sum(parts, r, up)
            if begun:
                a, u = a + acc[r, at], u + acc[r, up]
            hidden[r, at] = (a / (1.0 + jnp.exp(-a)) * u).astype(jnp.bfloat16)

    early = GATE_CHUNKS - 1
    cut = early * gsize
    far = (early - LAG) * gsize
    first = [(p, 0, depth), (pc, 0, cut), (3 - p, 0, cut), (3 - pc, 0, far)]
    last = [(pc, cut, depth - cut), (3 - p, cut, depth - cut), (3 - pc, far, depth - far)]
    whole = [(k, 0, depth) for k in (p, pc, 3 - p, 3 - pc)]

    for i in range(early):
        pass_on(i)

    @pl.when(native)
    def _():
        pltpu.make_async_copy(gate_hbm.at[0], gate.at[p], own_copy.at[0]).wait()
        pltpu.make_async_copy(down_hbm.at[0], down.at[p], own_copy.at[1]).wait()
        from_sibling(gate, 3 - p, gsize, range(early), gate_sa)
        from_sibling(gate, 3 - pc, gsize, range(early - LAG), gate_sb)

    @pl.when(foreign)
    def _():
        from_sibling(gate, p, gsize, range(GATE_CHUNKS), gate_sa)
        from_sibling(gate, pc, gsize, range(early), gate_sb)

    rows_in(0)
    rows_in(1)
    gate_begin(first, slice(0, 256))
    send_down()

    for i in range(early, GATE_CHUNKS):
        pass_on(i)

    @pl.when(native)
    def _():
        from_sibling(gate, 3 - p, gsize, range(early, GATE_CHUNKS), gate_sa)
        from_sibling(gate, 3 - pc, gsize, range(early - LAG, GATE_CHUNKS), gate_sb)

    @pl.when(foreign)
    def _():
        for i in range(GATE_CHUNKS - LAG, GATE_CHUNKS):
            share_far(i)
        from_sibling(gate, pc, gsize, range(early, GATE_CHUNKS), gate_sb)

    gate_finish(last, slice(0, 256), True)

    def quarter(k, halves):
        for half in halves:
            part = jnp.dot(hidden[half * 256 : half * 256 + 256, :], down[k], preferred_element_type=jnp.float32)
            result[k, half * 32 : half * 32 + 32] = part.astype(jnp.bfloat16).reshape(32, SLOTS, cols)
            for grp in (2 * half, 2 * half + 1):

                @pl.loop(0, 16)
                def _(i, grp=grp):
                    zsel, cs, ddx = i % 2, (i // 2) % 2, i // 4
                    ddz = DZ0[grp] + (DZ1[grp] - DZ0[grp]) * zsel
                    to = ((z + NZ - ddz) % NZ * 4 + (x + NX - ddx) % NX) * 2 + cs
                    bb = jnp.where(native, 0, 1)
                    src = result.at[k, grp * 16 + i]
                    dst = returned.at[k, grp * 16 + i + 2 * (bb - cs)]

                    def go():
                        remote(src, dst, ret_send, ret_recv.at[k], (home, to)).start()

                    if grp == 1:
                        own = native & (zsel == 1) & (ddx == 0) & (cs == c)

                        @pl.when(own)
                        def _():
                            pltpu.make_async_copy(src, dst, ret_recv.at[k]).start()

                        @pl.when(jnp.logical_not(own))
                        def _():
                            go()
                    else:
                        go()

    @pl.when(foreign)
    def _():
        from_sibling(down, p, dsize, range(DOWN_CHUNKS), down_sa)

    def pass_down(chunks):
        for i in chunks:
            arrived(down, 3 - p, i, dsize, down_in)
            forward(down, 3 - p, i, dsize, down_send, down_x, cross)
            forward(down, 3 - p, i, dsize, down_send, down_sa, sibling)

    quarter(p, (0,))
    rows_in(2)
    rows_in(3)
    gate_finish(whole, slice(256, 512), False)
    quarter(p, (1,))

    half = DOWN_CHUNKS // 2

    @pl.when(native)
    def _():
        for i in range(DOWN_CHUNKS):
            arrived(down, pc, i, dsize, down_in)
            forward(down, pc, i, dsize, down_send, down_sb, sibling)

    @pl.when(foreign)
    def _():
        pass_down(range(half))
        from_sibling(down, pc, dsize, range(DOWN_CHUNKS), down_sb)

    quarter(pc, (0, 1))

    @pl.when(native)
    def _():
        from_sibling(down, 3 - p, dsize, range(DOWN_CHUNKS), down_sa)

    @pl.when(foreign)
    def _():
        pass_down(range(half, DOWN_CHUNKS))

    quarter(3 - p, (0, 1))

    @pl.when(foreign)
    def _():
        for i in range(DOWN_CHUNKS):
            arrived(down, 3 - pc, i, dsize, down_x)
            forward(down, 3 - pc, i, dsize, down_send, down_sb, sibling)

    @pl.when(native)
    def _():
        from_sibling(down, 3 - pc, dsize, range(DOWN_CHUNKS), down_sb)

    quarter(3 - pc, (0, 1))

    for k in (p, 3 - p, pc, 3 - pc):
        pltpu.make_async_copy(returned.at[k], returned.at[k], ret_recv.at[k]).wait()
        mixed = jnp.dot(comb[...], returned[k].reshape(512, cols), preferred_element_type=jnp.float32)
        out_ref[:, pl.ds(pl.multiple_of(k * cols, 128), cols)] = mixed.astype(jnp.bfloat16)

    def sent(ref, sem):
        pltpu.make_async_copy(ref, ref, sem).wait()

    @pl.when(native)
    def _():
        sent(outgoing.at[pl.ds(0, 63)], disp_send)
        sent(gate.at[pl.ds(0, 3)], gate_send)
        sent(down.at[pl.ds(0, 3)], down_send)
        sent(result.at[pl.ds(0, 3)], ret_send)
        sent(result.at[3, pl.ds(0, 60)], ret_send)

    @pl.when(foreign)
    def _():
        sent(outgoing, disp_send)
        sent(gate, gate_send)
        sent(down, down_send)
        sent(result, ret_send)


def local(tokens, gate_up, down_proj, expert_ids, gate_weights):
    tok_rows, width = tokens.shape
    _, depth, wide = gate_up.shape
    _, ff, cols = down_proj.shape
    bf, f32 = jnp.bfloat16, jnp.float32
    vmem = pl.BlockSpec(memory_space=pltpu.VMEM)
    hbm = pl.BlockSpec(memory_space=pl.ANY)
    dma = pltpu.SemaphoreType.DMA
    return pl.pallas_call(
        kernel,
        out_shape=jax.ShapeDtypeStruct((tok_rows, width), bf),
        in_specs=[vmem, hbm, hbm, vmem, vmem],
        out_specs=vmem,
        scratch_shapes=[
            pltpu.VMEM((512, 128), bf),
            pltpu.VMEM((128, 512), bf),
            pltpu.VMEM((64, SLOTS, width), bf),
            pltpu.VMEM((64, SLOTS, width), bf),
            pltpu.VMEM((512, width), bf),
            pltpu.VMEM((4, depth, wide), bf),
            pltpu.VMEM((4, ff, cols), bf),
            pltpu.VMEM((512, wide), f32),
            pltpu.VMEM((512, ff), bf),
            pltpu.VMEM((4, 64, SLOTS, cols), bf),
            pltpu.VMEM((4, 64, SLOTS, cols), bf),
            dma, dma((GROUPS,)), dma((2,)),
            dma, dma((GATE_CHUNKS,)), dma((GATE_CHUNKS,)), dma((GATE_CHUNKS,)), dma((GATE_CHUNKS,)),
            dma, dma((DOWN_CHUNKS,)), dma((DOWN_CHUNKS,)), dma((DOWN_CHUNKS,)), dma((DOWN_CHUNKS,)),
            dma, dma((4,)),
        ],
        compiler_params=pltpu.CompilerParams(
            collective_id=0, has_side_effects=True, vmem_limit_bytes=60 * 1024 * 1024
        ),
    )(tokens, gate_up, down_proj, expert_ids, gate_weights)


def solution(mesh):
    placed = (
        P(("dp", "expert"), None),
        P("expert", "dp", None),
        P("expert", None, "dp"),
        P(("dp", "expert"), None),
        P(("dp", "expert"), None),
    )
    return jax.shard_map(
        local, mesh=mesh, in_specs=placed, out_specs=P(("dp", "expert"), None), check_vma=False
    )
```

```python
import functools

import jax
import jax.numpy as jnp
from jax import lax
from jax.experimental import pallas as pl
from jax.experimental.pallas import tpu as pltpu
from jax.sharding import PartitionSpec as P

MESH = pl.DeviceIdType.MESH
NZ, NX = 8, 4
SLOTS = 8
GROUPS = 4
DZ0 = (3, 4, 2, 1)
DZ1 = (5, 0, 6, 7)
GATE_CHUNKS = 7
DOWN_CHUNKS = 4
AHEAD = 7
LAG = 1
DISPATCH = (16, 32, 32, 48, 64, 64, 64, 64)


def kernel(
    tok_ref, gate_hbm, down_hbm, ids_ref, wts_ref, out_ref,
    place, comb, outgoing, rows, rows2, gate, down, acc, hidden, result, returned,
    disp_send, disp_recv, own_copy, gate_send, gate_in, gate_x, gate_sa, gate_sb,
    down_send, down_in, down_x, down_sa, down_sb, ret_send, ret_recv,
):
    p = lax.axis_index("dp")
    e = lax.axis_index("expert")
    z, x, c = e // 8, (e // 2) % 4, e % 2
    m = p // 2
    native = c == m
    foreign = c != m
    sibling = (p, e + 1 - 2 * c)
    pc = p + 1 - 2 * (p % 2)
    cross = (pc, e)
    across = (3 - p, e + 1 - 2 * c)
    home = jnp.where(native, p, 3 - p)
    ff = hidden.shape[1]
    depth = gate.shape[1]
    cols = down.shape[2]

    barrier = pltpu.get_barrier_semaphore()

    def greet(plane, to):
        pl.semaphore_signal(barrier, inc=1, device_id=(plane, to), device_id_type=MESH)

    for ddz in (4, 3, 5, 2, 6, 1, 7, 0):
        for ddx in (2, 1, 3, 0):
            chip = ((z + ddz) % NZ * 4 + (x + ddx) % NX) * 2
            greet(3 - p, chip + m)
            greet(home, chip + 1 - m)
            if ddz or ddx:
                greet(p, chip + m)
    greet(*cross)

    @pl.when(foreign)
    def _():
        greet(*sibling)

    row = lax.broadcasted_iota(jnp.int32, (512, 128), 0)
    g, ii = row // 128, (row // 8) % 16
    zs, b, dx = ii % 2, (ii // 2) % 2, ii // 4
    dz0 = jnp.where(g == 0, DZ0[0], jnp.where(g == 1, DZ0[1], jnp.where(g == 2, DZ0[2], DZ0[3])))
    dz1 = jnp.where(g == 0, DZ1[0], jnp.where(g == 1, DZ1[1], jnp.where(g == 2, DZ1[2], DZ1[3])))
    dz = jnp.where(zs == 0, dz0, dz1)
    core = jnp.where(b == 0, m, 1 - m)
    expert = ((z + dz) % NZ * 4 + (x + dx) % NX) * 2 + core
    ids = ids_ref[...]
    wts = wts_ref[...].astype(jnp.float32)
    named = jnp.zeros((512, 128), jnp.float32)
    weight = jnp.zeros((512, 128), jnp.float32)
    for k in range(8):
        same = expert == ids[k : k + 1, :]
        named = jnp.where(same, 1.0, named)
        weight = jnp.where(same, wts[k : k + 1, :], weight)
    t0 = lax.broadcasted_iota(jnp.int32, (128, 128), 0)
    t1 = lax.broadcasted_iota(jnp.int32, (128, 128), 1)
    earlier = jnp.where(t0 < t1, 1.0, 0.0).astype(jnp.bfloat16)
    before = jnp.dot(named.astype(jnp.bfloat16), earlier, preferred_element_type=jnp.float32)
    slot = (row % 8).astype(jnp.float32)
    chosen = (named > 0.5) & (before == slot)
    place[...] = jnp.where(chosen, 1.0, 0.0).astype(jnp.bfloat16)
    comb[...] = jnp.where(chosen, weight, 0.0).T.astype(jnp.bfloat16)

    def pick(r0, r1):
        @pl.loop(0, 7)
        def _(n):
            at = pl.ds(pl.multiple_of(n * 512, 512), 512)
            block = jnp.dot(place[r0:r1, :], tok_ref[:, at], preferred_element_type=jnp.float32)
            outgoing[r0 // 8 : r1 // 8, :, at] = block.astype(jnp.bfloat16).reshape((r1 - r0) // 8, SLOTS, 512)

    pick(0, 128)
    pl.semaphore_wait(barrier, jnp.where(native, 96, 97))

    def remote(src, dst, ssem, rsem, to):
        return pltpu.make_async_remote_copy(
            src_ref=src, dst_ref=dst, send_sem=ssem, recv_sem=rsem, device_id=to, device_id_type=MESH
        )

    def piece(ref, k, i, size):
        return ref.at[k, pl.ds(i * size, size), :]

    gsize, dsize = depth // GATE_CHUNKS, ff // DOWN_CHUNKS

    def send_own(hbm, dst, size, chunks, ssem, arrive, to):
        for i in chunks:
            remote(piece(hbm, 0, i, size), piece(dst, p, i, size), ssem, arrive.at[i], to).start()

    def forward(ref, k, i, size, ssem, arrive, to):
        remote(piece(ref, k, i, size), piece(ref, k, i, size), ssem, arrive.at[i], to).start()

    def arrived(ref, k, i, size, sem):
        pltpu.make_async_copy(piece(ref, k, i, size), piece(ref, k, i, size), sem.at[i]).wait()

    def send_gate(chunks):
        @pl.when(native)
        def _():
            send_own(gate_hbm, gate, gsize, chunks, gate_send, gate_in, cross)
            send_own(gate_hbm, gate, gsize, chunks, gate_send, gate_sa, sibling)

        @pl.when(foreign)
        def _():
            send_own(gate_hbm, gate, gsize, chunks, gate_send, gate_in, across)

    send_gate(range(AHEAD))

    def dispatch_part(grp, lo, hi):
        @pl.loop(lo, hi)
        def _(i):
            zsel, bb, ddx = i % 2, (i // 2) % 2, i // 4
            ddz = DZ0[grp] + (DZ1[grp] - DZ0[grp]) * zsel
            to = ((z + ddz) % NZ * 4 + (x + ddx) % NX) * 2 + m
            plane = p + bb * (3 - 2 * p)
            src = outgoing.at[grp * 16 + i]
            dst = rows.at[grp * 16 + i + 2 * (c - bb)]

            def go():
                remote(src, dst, disp_send, disp_recv.at[grp], (plane, to)).start()

            if grp == 1:
                own = native & (i == 1)

                @pl.when(own)
                def _():
                    pltpu.make_async_copy(src, dst, disp_recv.at[grp]).start()

                @pl.when(jnp.logical_not(own))
                def _():
                    go()
            else:
                go()

    def dispatch(lo, hi):
        for grp in range(GROUPS):
            if max(lo, grp * 16) < min(hi, grp * 16 + 16):
                dispatch_part(grp, max(lo - grp * 16, 0), min(hi - grp * 16, 16))

    dispatch(0, 16)
    pick(128, 512)
    dispatch(16, DISPATCH[0])

    @pl.when(native)
    def _():
        pltpu.make_async_copy(gate_hbm.at[0], gate.at[p], own_copy.at[0]).start()
        pltpu.make_async_copy(down_hbm.at[0], down.at[p], own_copy.at[1]).start()
        send_own(down_hbm, down, dsize, range(DOWN_CHUNKS), down_send, down_sa, sibling)

    def share_far(i):
        arrived(gate, 3 - pc, i, gsize, gate_x)
        forward(gate, 3 - pc, i, gsize, gate_send, gate_sb, sibling)

    def pass_on(i):
        if i + AHEAD < GATE_CHUNKS:
            send_gate([i + AHEAD])

        @pl.when(native)
        def _():
            arrived(gate, pc, i, gsize, gate_in)
            forward(gate, pc, i, gsize, gate_send, gate_sb, sibling)

        @pl.when(foreign)
        def _():
            arrived(gate, 3 - p, i, gsize, gate_in)
            forward(gate, 3 - p, i, gsize, gate_send, gate_x, cross)
            forward(gate, 3 - p, i, gsize, gate_send, gate_sa, sibling)
            if i >= LAG:
                share_far(i - LAG)

        dispatch(DISPATCH[i], DISPATCH[i + 1])

    def send_down():
        @pl.when(native)
        def _():
            send_own(down_hbm, down, dsize, range(DOWN_CHUNKS), down_send, down_in, cross)

        @pl.when(foreign)
        def _():
            send_own(down_hbm, down, dsize, range(DOWN_CHUNKS), down_send, down_in, across)

    def from_sibling(ref, k, size, chunks, sem):
        for i in chunks:
            arrived(ref, k, i, size, sem)

    def rows_in(grp):
        part = rows.at[pl.ds(grp * 16, 16)]
        pltpu.make_async_copy(part, part, disp_recv.at[grp]).wait()

        @pl.loop(0, 7)
        def _(n):
            at = pl.ds(pl.multiple_of(n * 512, 512), 512)
            rows2[grp * 128 : grp * 128 + 128, at] = rows[grp * 16 : grp * 16 + 16, :, at].reshape(128, 512)

    def gate_sum(parts, r, at):
        total = None
        for k, k0, kd in parts:
            deep = pl.ds(pl.multiple_of(k * depth + k0, 128), kd)
            term = jnp.dot(rows2[r, deep], gate[k, k0 : k0 + kd, at], preferred_element_type=jnp.float32)
            total = term if total is None else total + term
        return total

    def gate_begin(parts, r):
        @pl.loop(0, 2 * ff // 256)
        def _(n):
            at = pl.ds(pl.multiple_of(n * 256, 256), 256)
            acc[r, at] = gate_sum(parts, r, at)

    def gate_finish(parts, r, begun):
        @pl.loop(0, ff // 256)
        def _(n):
            at = pl.ds(pl.multiple_of(n * 256, 256), 256)
            up = pl.ds(pl.multiple_of(ff + n * 256, 256), 256)
            a, u = gate_sum(parts, r, at), gate_sum(parts, r, up)
            if begun:
                a, u = a + acc[r, at], u + acc[r, up]
            hidden[r, at] = (a / (1.0 + jnp.exp(-a)) * u).astype(jnp.bfloat16)

    early = GATE_CHUNKS - 1
    cut = early * gsize
    far = (early - LAG) * gsize
    first = [(p, 0, depth), (pc, 0, cut), (3 - p, 0, cut), (3 - pc, 0, far)]
    last = [(pc, cut, depth - cut), (3 - p, cut, depth - cut), (3 - pc, far, depth - far)]
    whole = [(k, 0, depth) for k in (p, pc, 3 - p, 3 - pc)]

    for i in range(early):
        pass_on(i)

    @pl.when(native)
    def _():
        pltpu.make_async_copy(gate_hbm.at[0], gate.at[p], own_copy.at[0]).wait()
        pltpu.make_async_copy(down_hbm.at[0], down.at[p], own_copy.at[1]).wait()
        from_sibling(gate, 3 - p, gsize, range(early), gate_sa)
        from_sibling(gate, 3 - pc, gsize, range(early - LAG), gate_sb)

    @pl.when(foreign)
    def _():
        from_sibling(gate, p, gsize, range(GATE_CHUNKS), gate_sa)
        from_sibling(gate, pc, gsize, range(early), gate_sb)

    rows_in(0)
    rows_in(1)
    gate_begin(first, slice(0, 256))
    send_down()

    for i in range(early, GATE_CHUNKS):
        pass_on(i)

    @pl.when(native)
    def _():
        from_sibling(gate, 3 - p, gsize, range(early, GATE_CHUNKS), gate_sa)
        from_sibling(gate, 3 - pc, gsize, range(early - LAG, GATE_CHUNKS), gate_sb)

    @pl.when(foreign)
    def _():
        for i in range(GATE_CHUNKS - LAG, GATE_CHUNKS):
            share_far(i)
        from_sibling(gate, pc, gsize, range(early, GATE_CHUNKS), gate_sb)

    gate_finish(last, slice(0, 256), True)

    def quarter(k, halves):
        for half in halves:
            part = jnp.dot(hidden[half * 256 : half * 256 + 256, :], down[k], preferred_element_type=jnp.float32)
            result[k, half * 32 : half * 32 + 32] = part.astype(jnp.bfloat16).reshape(32, SLOTS, cols)
            for grp in (2 * half, 2 * half + 1):

                @pl.loop(0, 16)
                def _(i, grp=grp):
                    zsel, cs, ddx = i % 2, (i // 2) % 2, i // 4
                    ddz = DZ0[grp] + (DZ1[grp] - DZ0[grp]) * zsel
                    to = ((z + NZ - ddz) % NZ * 4 + (x + NX - ddx) % NX) * 2 + cs
                    bb = jnp.where(native, 0, 1)
                    src = result.at[k, grp * 16 + i]
                    dst = returned.at[k, grp * 16 + i + 2 * (bb - cs)]

                    def go():
                        remote(src, dst, ret_send, ret_recv.at[k], (home, to)).start()

                    if grp == 1:
                        own = native & (zsel == 1) & (ddx == 0) & (cs == c)

                        @pl.when(own)
                        def _():
                            pltpu.make_async_copy(src, dst, ret_recv.at[k]).start()

                        @pl.when(jnp.logical_not(own))
                        def _():
                            go()
                    else:
                        go()

    @pl.when(foreign)
    def _():
        from_sibling(down, p, dsize, range(DOWN_CHUNKS), down_sa)

    def pass_down(chunks):
        for i in chunks:
            arrived(down, 3 - p, i, dsize, down_in)
            forward(down, 3 - p, i, dsize, down_send, down_x, cross)
            forward(down, 3 - p, i, dsize, down_send, down_sa, sibling)

    quarter(p, (0,))
    rows_in(2)
    rows_in(3)
    gate_finish(whole, slice(256, 512), False)
    quarter(p, (1,))

    half = DOWN_CHUNKS // 2

    @pl.when(native)
    def _():
        for i in range(DOWN_CHUNKS):
            arrived(down, pc, i, dsize, down_in)
            forward(down, pc, i, dsize, down_send, down_sb, sibling)

    @pl.when(foreign)
    def _():
        pass_down(range(half))
        from_sibling(down, pc, dsize, range(DOWN_CHUNKS), down_sb)

    quarter(pc, (0, 1))

    @pl.when(native)
    def _():
        from_sibling(down, 3 - p, dsize, range(DOWN_CHUNKS), down_sa)

    @pl.when(foreign)
    def _():
        pass_down(range(half, DOWN_CHUNKS))

    quarter(3 - p, (0, 1))

    @pl.when(foreign)
    def _():
        for i in range(DOWN_CHUNKS):
            arrived(down, 3 - pc, i, dsize, down_x)
            forward(down, 3 - pc, i, dsize, down_send, down_sb, sibling)

    @pl.when(native)
    def _():
        from_sibling(down, 3 - pc, dsize, range(DOWN_CHUNKS), down_sb)

    quarter(3 - pc, (0, 1))

    for k in (p, 3 - p, pc, 3 - pc):
        pltpu.make_async_copy(returned.at[k], returned.at[k], ret_recv.at[k]).wait()
        mixed = jnp.dot(comb[...], returned[k].reshape(512, cols), preferred_element_type=jnp.float32)
        out_ref[:, pl.ds(pl.multiple_of(k * cols, 128), cols)] = mixed.astype(jnp.bfloat16)

    def sent(ref, sem):
        pltpu.make_async_copy(ref, ref, sem).wait()

    @pl.when(native)
    def _():
        sent(outgoing.at[pl.ds(0, 63)], disp_send)
        sent(gate.at[pl.ds(0, 3)], gate_send)
        sent(down.at[pl.ds(0, 3)], down_send)
        sent(result.at[pl.ds(0, 3)], ret_send)
        sent(result.at[3, pl.ds(0, 60)], ret_send)

    @pl.when(foreign)
    def _():
        sent(outgoing, disp_send)
        sent(gate, gate_send)
        sent(down, down_send)
        sent(result, ret_send)


def local(tokens, gate_up, down_proj, expert_ids, gate_weights):
    tok_rows, width = tokens.shape
    _, depth, wide = gate_up.shape
    _, ff, cols = down_proj.shape
    bf, f32 = jnp.bfloat16, jnp.float32
    vmem = pl.BlockSpec(memory_space=pltpu.VMEM)
    hbm = pl.BlockSpec(memory_space=pl.ANY)
    dma = pltpu.SemaphoreType.DMA
    return pl.pallas_call(
        kernel,
        out_shape=jax.ShapeDtypeStruct((tok_rows, width), bf),
        in_specs=[vmem, hbm, hbm, vmem, vmem],
        out_specs=vmem,
        scratch_shapes=[
            pltpu.VMEM((512, 128), bf),
            pltpu.VMEM((128, 512), bf),
            pltpu.VMEM((64, SLOTS, width), bf),
            pltpu.VMEM((64, SLOTS, width), bf),
            pltpu.VMEM((512, width), bf),
            pltpu.VMEM((4, depth, wide), bf),
            pltpu.VMEM((4, ff, cols), bf),
            pltpu.VMEM((512, wide), f32),
            pltpu.VMEM((512, ff), bf),
            pltpu.VMEM((4, 64, SLOTS, cols), bf),
            pltpu.VMEM((4, 64, SLOTS, cols), bf),
            dma, dma((GROUPS,)), dma((2,)),
            dma, dma((GATE_CHUNKS,)), dma((GATE_CHUNKS,)), dma((GATE_CHUNKS,)), dma((GATE_CHUNKS,)),
            dma, dma((DOWN_CHUNKS,)), dma((DOWN_CHUNKS,)), dma((DOWN_CHUNKS,)), dma((DOWN_CHUNKS,)),
            dma, dma((4,)),
        ],
        compiler_params=pltpu.CompilerParams(
            collective_id=0, has_side_effects=True, vmem_limit_bytes=60 * 1024 * 1024
        ),
    )(tokens, gate_up, down_proj, expert_ids.T, gate_weights.T)


def solution(mesh):
    placed = (
        P(("dp", "expert"), None),
        P("expert", "dp", None),
        P("expert", None, "dp"),
        P(("dp", "expert"), None),
        P(("dp", "expert"), None),
    )
    return jax.shard_map(
        local, mesh=mesh, in_specs=placed, out_specs=P(("dp", "expert"), None), check_vma=False
    )
```

```python
import functools

import jax
import jax.numpy as jnp
from jax import lax
from jax.experimental import pallas as pl
from jax.experimental.pallas import tpu as pltpu
from jax.sharding import PartitionSpec as P

MESH = pl.DeviceIdType.MESH
NZ, NX = 8, 4
SLOTS = 8
GROUPS = 4
DZ0 = (3, 4, 2, 1)
DZ1 = (5, 0, 6, 7)
GATE_CHUNKS = 7
DOWN_CHUNKS = 4
AHEAD = 7
LAG = 1
DISPATCH = (16, 32, 32, 48, 64, 64, 64, 64)


def kernel(
    tok_hbm, gate_hbm, down_hbm, ids_ref, wts_ref, out_ref,
    place, comb, outgoing, rows, rows2, gate, down, acc, hidden, result, returned,
    disp_send, disp_recv, own_copy, gate_send, gate_in, gate_x, gate_sa, gate_sb,
    down_send, down_in, down_x, down_sa, down_sb, ret_send, ret_recv,
    tok_ref, tok_sem,
):
    p = lax.axis_index("dp")
    e = lax.axis_index("expert")
    z, x, c = e // 8, (e // 2) % 4, e % 2
    m = p // 2
    native = c == m
    foreign = c != m
    sibling = (p, e + 1 - 2 * c)
    pc = p + 1 - 2 * (p % 2)
    cross = (pc, e)
    across = (3 - p, e + 1 - 2 * c)
    home = jnp.where(native, p, 3 - p)
    ff = hidden.shape[1]
    depth = gate.shape[1]
    cols = down.shape[2]

    tok_copy = pltpu.make_async_copy(tok_hbm, tok_ref, tok_sem)
    tok_copy.start()

    barrier = pltpu.get_barrier_semaphore()

    def greet(plane, to):
        pl.semaphore_signal(barrier, inc=1, device_id=(plane, to), device_id_type=MESH)

    for ddz in (4, 3, 5, 2, 6, 1, 7, 0):
        for ddx in (2, 1, 3, 0):
            chip = ((z + ddz) % NZ * 4 + (x + ddx) % NX) * 2
            greet(3 - p, chip + m)
            greet(home, chip + 1 - m)
            if ddz or ddx:
                greet(p, chip + m)
    greet(*cross)

    @pl.when(foreign)
    def _():
        greet(*sibling)

    row = lax.broadcasted_iota(jnp.int32, (512, 128), 0)
    g, ii = row // 128, (row // 8) % 16
    zs, b, dx = ii % 2, (ii // 2) % 2, ii // 4
    dz0 = jnp.where(g == 0, DZ0[0], jnp.where(g == 1, DZ0[1], jnp.where(g == 2, DZ0[2], DZ0[3])))
    dz1 = jnp.where(g == 0, DZ1[0], jnp.where(g == 1, DZ1[1], jnp.where(g == 2, DZ1[2], DZ1[3])))
    dz = jnp.where(zs == 0, dz0, dz1)
    core = jnp.where(b == 0, m, 1 - m)
    expert = ((z + dz) % NZ * 4 + (x + dx) % NX) * 2 + core
    ids = ids_ref[...]
    wts = wts_ref[...].astype(jnp.float32)
    named = jnp.zeros((512, 128), jnp.float32)
    weight = jnp.zeros((512, 128), jnp.float32)
    for k in range(8):
        same = expert == ids[k : k + 1, :]
        named = jnp.where(same, 1.0, named)
        weight = jnp.where(same, wts[k : k + 1, :], weight)
    t0 = lax.broadcasted_iota(jnp.int32, (128, 128), 0)
    t1 = lax.broadcasted_iota(jnp.int32, (128, 128), 1)
    earlier = jnp.where(t0 < t1, 1.0, 0.0).astype(jnp.bfloat16)
    before = jnp.dot(named.astype(jnp.bfloat16), earlier, preferred_element_type=jnp.float32)
    slot = (row % 8).astype(jnp.float32)
    chosen = (named > 0.5) & (before == slot)
    place[...] = jnp.where(chosen, 1.0, 0.0).astype(jnp.bfloat16)
    comb[...] = jnp.where(chosen, weight, 0.0).T.astype(jnp.bfloat16)

    def pick(r0, r1):
        @pl.loop(0, 7)
        def _(n):
            at = pl.ds(pl.multiple_of(n * 512, 512), 512)
            block = jnp.dot(place[r0:r1, :], tok_ref[:, at], preferred_element_type=jnp.float32)
            outgoing[r0 // 8 : r1 // 8, :, at] = block.astype(jnp.bfloat16).reshape((r1 - r0) // 8, SLOTS, 512)

    tok_copy.wait()
    pick(0, 128)
    pl.semaphore_wait(barrier, jnp.where(native, 96, 97))

    def remote(src, dst, ssem, rsem, to):
        return pltpu.make_async_remote_copy(
            src_ref=src, dst_ref=dst, send_sem=ssem, recv_sem=rsem, device_id=to, device_id_type=MESH
        )

    def piece(ref, k, i, size):
        return ref.at[k, pl.ds(i * size, size), :]

    gsize, dsize = depth // GATE_CHUNKS, ff // DOWN_CHUNKS

    def send_own(hbm, dst, size, chunks, ssem, arrive, to):
        for i in chunks:
            remote(piece(hbm, 0, i, size), piece(dst, p, i, size), ssem, arrive.at[i], to).start()

    def forward(ref, k, i, size, ssem, arrive, to):
        remote(piece(ref, k, i, size), piece(ref, k, i, size), ssem, arrive.at[i], to).start()

    def arrived(ref, k, i, size, sem):
        pltpu.make_async_copy(piece(ref, k, i, size), piece(ref, k, i, size), sem.at[i]).wait()

    def send_gate(chunks):
        @pl.when(native)
        def _():
            send_own(gate_hbm, gate, gsize, chunks, gate_send, gate_in, cross)
            send_own(gate_hbm, gate, gsize, chunks, gate_send, gate_sa, sibling)

        @pl.when(foreign)
        def _():
            send_own(gate_hbm, gate, gsize, chunks, gate_send, gate_in, across)

    send_gate(range(AHEAD))

    def dispatch_part(grp, lo, hi):
        @pl.loop(lo, hi)
        def _(i):
            zsel, bb, ddx = i % 2, (i // 2) % 2, i // 4
            ddz = DZ0[grp] + (DZ1[grp] - DZ0[grp]) * zsel
            to = ((z + ddz) % NZ * 4 + (x + ddx) % NX) * 2 + m
            plane = p + bb * (3 - 2 * p)
            src = outgoing.at[grp * 16 + i]
            dst = rows.at[grp * 16 + i + 2 * (c - bb)]

            def go():
                remote(src, dst, disp_send, disp_recv.at[grp], (plane, to)).start()

            if grp == 1:
                own = native & (i == 1)

                @pl.when(own)
                def _():
                    pltpu.make_async_copy(src, dst, disp_recv.at[grp]).start()

                @pl.when(jnp.logical_not(own))
                def _():
                    go()
            else:
                go()

    def dispatch(lo, hi):
        for grp in range(GROUPS):
            if max(lo, grp * 16) < min(hi, grp * 16 + 16):
                dispatch_part(grp, max(lo - grp * 16, 0), min(hi - grp * 16, 16))

    dispatch(0, 16)
    pick(128, 512)
    dispatch(16, DISPATCH[0])

    @pl.when(native)
    def _():
        pltpu.make_async_copy(gate_hbm.at[0], gate.at[p], own_copy.at[0]).start()
        pltpu.make_async_copy(down_hbm.at[0], down.at[p], own_copy.at[1]).start()
        send_own(down_hbm, down, dsize, range(DOWN_CHUNKS), down_send, down_sa, sibling)

    def share_far(i):
        arrived(gate, 3 - pc, i, gsize, gate_x)
        forward(gate, 3 - pc, i, gsize, gate_send, gate_sb, sibling)

    def pass_on(i):
        if i + AHEAD < GATE_CHUNKS:
            send_gate([i + AHEAD])

        @pl.when(native)
        def _():
            arrived(gate, pc, i, gsize, gate_in)
            forward(gate, pc, i, gsize, gate_send, gate_sb, sibling)

        @pl.when(foreign)
        def _():
            arrived(gate, 3 - p, i, gsize, gate_in)
            forward(gate, 3 - p, i, gsize, gate_send, gate_x, cross)
            forward(gate, 3 - p, i, gsize, gate_send, gate_sa, sibling)
            if i >= LAG:
                share_far(i - LAG)

        dispatch(DISPATCH[i], DISPATCH[i + 1])

    def send_down():
        @pl.when(native)
        def _():
            send_own(down_hbm, down, dsize, range(DOWN_CHUNKS), down_send, down_in, cross)

        @pl.when(foreign)
        def _():
            send_own(down_hbm, down, dsize, range(DOWN_CHUNKS), down_send, down_in, across)

    def from_sibling(ref, k, size, chunks, sem):
        for i in chunks:
            arrived(ref, k, i, size, sem)

    def rows_in(grp):
        part = rows.at[pl.ds(grp * 16, 16)]
        pltpu.make_async_copy(part, part, disp_recv.at[grp]).wait()

        @pl.loop(0, 7)
        def _(n):
            at = pl.ds(pl.multiple_of(n * 512, 512), 512)
            rows2[grp * 128 : grp * 128 + 128, at] = rows[grp * 16 : grp * 16 + 16, :, at].reshape(128, 512)

    def gate_sum(parts, r, at):
        total = None
        for k, k0, kd in parts:
            deep = pl.ds(pl.multiple_of(k * depth + k0, 128), kd)
            term = jnp.dot(rows2[r, deep], gate[k, k0 : k0 + kd, at], preferred_element_type=jnp.float32)
            total = term if total is None else total + term
        return total

    def gate_begin(parts, r):
        @pl.loop(0, 2 * ff // 256)
        def _(n):
            at = pl.ds(pl.multiple_of(n * 256, 256), 256)
            acc[r, at] = gate_sum(parts, r, at)

    def gate_finish(parts, r, begun):
        @pl.loop(0, ff // 256)
        def _(n):
            at = pl.ds(pl.multiple_of(n * 256, 256), 256)
            up = pl.ds(pl.multiple_of(ff + n * 256, 256), 256)
            a, u = gate_sum(parts, r, at), gate_sum(parts, r, up)
            if begun:
                a, u = a + acc[r, at], u + acc[r, up]
            hidden[r, at] = (a / (1.0 + jnp.exp(-a)) * u).astype(jnp.bfloat16)

    early = GATE_CHUNKS - 1
    cut = early * gsize
    far = (early - LAG) * gsize
    first = [(p, 0, depth), (pc, 0, cut), (3 - p, 0, cut), (3 - pc, 0, far)]
    last = [(pc, cut, depth - cut), (3 - p, cut, depth - cut), (3 - pc, far, depth - far)]
    whole = [(k, 0, depth) for k in (p, pc, 3 - p, 3 - pc)]

    for i in range(early):
        pass_on(i)

    @pl.when(native)
    def _():
        pltpu.make_async_copy(gate_hbm.at[0], gate.at[p], own_copy.at[0]).wait()
        pltpu.make_async_copy(down_hbm.at[0], down.at[p], own_copy.at[1]).wait()
        from_sibling(gate, 3 - p, gsize, range(early), gate_sa)
        from_sibling(gate, 3 - pc, gsize, range(early - LAG), gate_sb)

    @pl.when(foreign)
    def _():
        from_sibling(gate, p, gsize, range(GATE_CHUNKS), gate_sa)
        from_sibling(gate, pc, gsize, range(early), gate_sb)

    rows_in(0)
    rows_in(1)
    gate_begin(first, slice(0, 256))
    send_down()

    for i in range(early, GATE_CHUNKS):
        pass_on(i)

    @pl.when(native)
    def _():
        from_sibling(gate, 3 - p, gsize, range(early, GATE_CHUNKS), gate_sa)
        from_sibling(gate, 3 - pc, gsize, range(early - LAG, GATE_CHUNKS), gate_sb)

    @pl.when(foreign)
    def _():
        for i in range(GATE_CHUNKS - LAG, GATE_CHUNKS):
            share_far(i)
        from_sibling(gate, pc, gsize, range(early, GATE_CHUNKS), gate_sb)

    gate_finish(last, slice(0, 256), True)

    def quarter(k, halves):
        for half in halves:
            part = jnp.dot(hidden[half * 256 : half * 256 + 256, :], down[k], preferred_element_type=jnp.float32)
            result[k, half * 32 : half * 32 + 32] = part.astype(jnp.bfloat16).reshape(32, SLOTS, cols)
            for grp in (2 * half, 2 * half + 1):

                @pl.loop(0, 16)
                def _(i, grp=grp):
                    zsel, cs, ddx = i % 2, (i // 2) % 2, i // 4
                    ddz = DZ0[grp] + (DZ1[grp] - DZ0[grp]) * zsel
                    to = ((z + NZ - ddz) % NZ * 4 + (x + NX - ddx) % NX) * 2 + cs
                    bb = jnp.where(native, 0, 1)
                    src = result.at[k, grp * 16 + i]
                    dst = returned.at[k, grp * 16 + i + 2 * (bb - cs)]

                    def go():
                        remote(src, dst, ret_send, ret_recv.at[k], (home, to)).start()

                    if grp == 1:
                        own = native & (zsel == 1) & (ddx == 0) & (cs == c)

                        @pl.when(own)
                        def _():
                            pltpu.make_async_copy(src, dst, ret_recv.at[k]).start()

                        @pl.when(jnp.logical_not(own))
                        def _():
                            go()
                    else:
                        go()

    @pl.when(foreign)
    def _():
        from_sibling(down, p, dsize, range(DOWN_CHUNKS), down_sa)

    def pass_down(chunks):
        for i in chunks:
            arrived(down, 3 - p, i, dsize, down_in)
            forward(down, 3 - p, i, dsize, down_send, down_x, cross)
            forward(down, 3 - p, i, dsize, down_send, down_sa, sibling)

    quarter(p, (0,))
    rows_in(2)
    rows_in(3)
    gate_finish(whole, slice(256, 512), False)
    quarter(p, (1,))

    half = DOWN_CHUNKS // 2

    @pl.when(native)
    def _():
        for i in range(DOWN_CHUNKS):
            arrived(down, pc, i, dsize, down_in)
            forward(down, pc, i, dsize, down_send, down_sb, sibling)

    @pl.when(foreign)
    def _():
        pass_down(range(half))
        from_sibling(down, pc, dsize, range(DOWN_CHUNKS), down_sb)

    quarter(pc, (0, 1))

    @pl.when(native)
    def _():
        from_sibling(down, 3 - p, dsize, range(DOWN_CHUNKS), down_sa)

    @pl.when(foreign)
    def _():
        pass_down(range(half, DOWN_CHUNKS))

    quarter(3 - p, (0, 1))

    @pl.when(foreign)
    def _():
        for i in range(DOWN_CHUNKS):
            arrived(down, 3 - pc, i, dsize, down_x)
            forward(down, 3 - pc, i, dsize, down_send, down_sb, sibling)

    @pl.when(native)
    def _():
        from_sibling(down, 3 - pc, dsize, range(DOWN_CHUNKS), down_sb)

    quarter(3 - pc, (0, 1))

    for k in (p, 3 - p, pc, 3 - pc):
        pltpu.make_async_copy(returned.at[k], returned.at[k], ret_recv.at[k]).wait()
        mixed = jnp.dot(comb[...], returned[k].reshape(512, cols), preferred_element_type=jnp.float32)
        out_ref[:, pl.ds(pl.multiple_of(k * cols, 128), cols)] = mixed.astype(jnp.bfloat16)

    def sent(ref, sem):
        pltpu.make_async_copy(ref, ref, sem).wait()

    @pl.when(native)
    def _():
        sent(outgoing.at[pl.ds(0, 63)], disp_send)
        sent(gate.at[pl.ds(0, 3)], gate_send)
        sent(down.at[pl.ds(0, 3)], down_send)
        sent(result.at[pl.ds(0, 3)], ret_send)
        sent(result.at[3, pl.ds(0, 60)], ret_send)

    @pl.when(foreign)
    def _():
        sent(outgoing, disp_send)
        sent(gate, gate_send)
        sent(down, down_send)
        sent(result, ret_send)


def local(tokens, gate_up, down_proj, expert_ids, gate_weights):
    tok_rows, width = tokens.shape
    _, depth, wide = gate_up.shape
    _, ff, cols = down_proj.shape
    bf, f32 = jnp.bfloat16, jnp.float32
    vmem = pl.BlockSpec(memory_space=pltpu.VMEM)
    hbm = pl.BlockSpec(memory_space=pl.ANY)
    dma = pltpu.SemaphoreType.DMA
    return pl.pallas_call(
        kernel,
        out_shape=jax.ShapeDtypeStruct((tok_rows, width), bf),
        in_specs=[hbm, hbm, hbm, vmem, vmem],
        out_specs=vmem,
        scratch_shapes=[
            pltpu.VMEM((512, 128), bf),
            pltpu.VMEM((128, 512), bf),
            pltpu.VMEM((64, SLOTS, width), bf),
            pltpu.VMEM((64, SLOTS, width), bf),
            pltpu.VMEM((512, width), bf),
            pltpu.VMEM((4, depth, wide), bf),
            pltpu.VMEM((4, ff, cols), bf),
            pltpu.VMEM((512, wide), f32),
            pltpu.VMEM((512, ff), bf),
            pltpu.VMEM((4, 64, SLOTS, cols), bf),
            pltpu.VMEM((4, 64, SLOTS, cols), bf),
            dma, dma((GROUPS,)), dma((2,)),
            dma, dma((GATE_CHUNKS,)), dma((GATE_CHUNKS,)), dma((GATE_CHUNKS,)), dma((GATE_CHUNKS,)),
            dma, dma((DOWN_CHUNKS,)), dma((DOWN_CHUNKS,)), dma((DOWN_CHUNKS,)), dma((DOWN_CHUNKS,)),
            dma, dma((4,)),
            pltpu.VMEM((tok_rows, width), bf), dma,
        ],
        compiler_params=pltpu.CompilerParams(
            collective_id=0, has_side_effects=True, vmem_limit_bytes=60 * 1024 * 1024
        ),
    )(tokens, gate_up, down_proj, expert_ids.T, gate_weights.T)


def solution(mesh):
    placed = (
        P(("dp", "expert"), None),
        P("expert", "dp", None),
        P("expert", None, "dp"),
        P(("dp", "expert"), None),
        P(("dp", "expert"), None),
    )
    return jax.shard_map(
        local, mesh=mesh, in_specs=placed, out_specs=P(("dp", "expert"), None), check_vma=False
    )
```
